512 devices in a mesh: seq: 32 (over y, z_lo), mp: 16 (over x, z_hi, core).
Axes of the slice: x: 4, y: 4, z: 16 (z_hi: 2, z_lo: 8; z = z_hi * 8 + z_lo), core: 2. Of those that a mesh axis runs over, the one named last changes fastest.
Arguments:
- tokens: bfloat16 [4096, 8192], P('seq', 'mp'), may hold values from -6 to 6
- in_weight: bfloat16 [8192, 3, 4096], P('seq', None, 'mp'), may hold values from -0.0625 to 0.0625
- short_taps: float32 [3, 3, 4096], P(None, None, 'mp'), may hold values from -4 to 4
- carry_rows: bfloat16 [2, 3, 4096], P(None, None, 'mp'), may hold values from -6 to 6
- pole_rates: float32 [16, 16], replicated, may hold values from 3e-05 to 0.03
- residues: float32 [16, 16], replicated, may hold values from -0.1 to 0.1
- carry_state: float32 [4096, 16], P('mp'), may hold values from -60 to 60
- skip_gain: float32 [4096], P('mp'), may hold values from -4 to 4
- groups: int32 [4096], P('mp'), may hold values from 0 to 15
Outputs:
- result: bfloat16 [4096, 4096], P('seq', 'mp')
The draws below stay inside these ranges and needn't reach their ends.
All inputs are finite; a program needn't handle non-finite values.
Results may differ from the reference program's by a relative error of at most 0.008.
Values may be sent and summed in bfloat16 or wider, within the bound.
A program may use at most 128 MiB of HBM per device.

```python
import math
import jax
import jax.numpy as jnp
from jax import lax

D = 8192
C = 4096
G = 16
ORDER = 16
TAPS = 3
LEN = 4096


def plant(array, rng, least, top_value):
    longest = array.shape.index(max(array.shape))
    spots = []
    for shift in (0, 1):
        where = [jax.random.randint(jax.random.fold_in(rng, axis), (), 0, length) for axis, length in enumerate(array.shape)]
        where[longest] = (where[longest] + shift) % array.shape[longest]
        spots.append(tuple(where))
    return array.at[spots[0]].set(least).at[spots[1]].set(top_value)


def steps_of(key, dims, shards, smallest, largest):
    factor_of, own = 1.0, jax.random.fold_in(key, 6)
    for axis_at, shards_of in shards:
        heights = jnp.exp(jax.random.uniform(jax.random.fold_in(own, axis_at), (shards_of,), jnp.float32, smallest / len(shards), largest / len(shards)))
        factor_of = factor_of * jnp.repeat(heights, dims[axis_at] // shards_of).reshape([-1 if axis == axis_at else 1 for axis in range(len(dims))])
    return factor_of


def noise(key, dims, scale, limit, cuts=(), held_as=jnp.bfloat16):
    drawn = jax.random.normal(key, dims, jnp.float32) * scale
    if len(cuts) > 0:
        drawn = steps_of(key, dims, cuts, -0.22, 0.18) * drawn
    return jnp.clip(drawn, min=-limit, max=limit).astype(held_as)


def setup_inputs(seed: int = 0) -> dict:
    splits = jax.random.split(jax.random.key(seed), 10)
    return {
        "tokens": noise(splits[0], (LEN, D), 1.0, 6.0, ((0, 32), (1, 16))),
        "in_weight": noise(splits[1], (D, 3, C), D ** -0.5, 0.0625, ((0, 32), (2, 16))),
        "short_taps": noise(splits[2], (TAPS, 3, C), 0.8, 4.0, ((2, 16),), jnp.float32),
        "carry_rows": noise(splits[3], (TAPS - 1, 3, C), 1.0, 6.0, ((2, 16),)),
        "pole_rates": jnp.clip(jnp.exp(jax.random.uniform(splits[4], (G, ORDER), jnp.float32, math.log(2.9999999242136255e-05), math.log(0.03))), 2.9999999242136255e-05, 0.03),
        "residues": noise(splits[5], (G, ORDER), 0.02, 0.1, (), jnp.float32),
        "carry_state": noise(splits[6], (C, ORDER), 10.0, 60.0, ((0, 16),), jnp.float32),
        "skip_gain": noise(splits[7], (C,), 1.0, 4.0, ((0, 16),), jnp.float32),
        "groups": plant(jax.random.randint(splits[8], (C,), 0, G), jax.random.fold_in(splits[8], 1), 0, G - 1).astype(jnp.int32),
    }


def reference(tokens, in_weight, short_taps, carry_rows, pole_rates, residues, carry_state, skip_gain, groups):
    highest = lax.Precision.HIGHEST
    projected = jnp.dot(tokens, in_weight.reshape(D, 3 * C), preferred_element_type=jnp.float32)
    projected = projected.astype(jnp.bfloat16).reshape(LEN, 3, C)
    extended = jnp.concatenate([carry_rows, projected], axis=0).astype(jnp.float32)
    short_mix = short_taps[0] * extended[2:] + short_taps[1] * extended[1:-1] + short_taps[2] * extended[:-2]
    query_rows = short_mix[:, 0]
    gated_rows = (short_mix[:, 1] * short_mix[:, 2]).astype(jnp.bfloat16)
    one_hot = (groups[:, None] == jnp.arange(G, dtype=jnp.int32)[None, :]).astype(jnp.float32)
    chan_res = jnp.dot(one_hot, residues, precision=highest)
    positions = jnp.arange(LEN).astype(jnp.float32)
    group_kernel = jnp.sum(residues[:, :, None] * jnp.exp(-pole_rates[:, :, None] * positions), axis=1)
    kernel = jnp.dot(one_hot, group_kernel, precision=highest)
    signal = gated_rows.astype(jnp.float32).T
    spectrum = jnp.fft.rfft(signal, n=2 * LEN, axis=1) * jnp.fft.rfft(kernel, n=2 * LEN, axis=1)
    conv_long = jnp.fft.irfft(spectrum, n=2 * LEN, axis=1)[:, :LEN]
    weights_mix = (one_hot[:, :, None] * (chan_res * carry_state)[:, None, :]).reshape(C, G * ORDER)
    decay_table = jnp.exp(-pole_rates[:, :, None] * (positions + 1.0)).reshape(G * ORDER, LEN)
    carried_part = jnp.dot(weights_mix, decay_table, precision=highest)
    long_mixed = (conv_long + carried_part).astype(jnp.bfloat16)
    long_mixed = lax.optimization_barrier(long_mixed)
    result = query_rows * (long_mixed.T.astype(jnp.float32) + skip_gain * gated_rows.astype(jnp.float32))
    return result.astype(jnp.bfloat16)
```

```python
import functools

import jax
import jax.numpy as jnp
from jax import lax
from jax.experimental import pallas as pl
from jax.experimental.pallas import tpu as pltpu
from jax.sharding import PartitionSpec as P

MESH = pl.DeviceIdType.MESH
SUBS = 2
STAGE_TWO, SPREAD, FORWARD = 2, 5, 7


def device(x, y, z, c):
    return {"seq": y * 8 + z % 8, "mp": x * 4 + (z // 8) * 2 + c}


def kernel(
    tok_ref,
    w_ref,
    prm_ref,
    modes_ref,
    out_ref,
    a_buf,
    stage_buf,
    w_buf,
    part_buf,
    sum_buf,
    prm_buf,
    ext_buf,
    gated_buf,
    query_buf,
    long_buf,
    state_buf,
    halo_send,
    halo_recv,
    home_send,
    home_recv,
    ring_s,
    ring_r,
    sib_s,
    sib_r,
    one_s,
    one_r,
    two_s,
    two_r,
    col_s,
    col_r,
    sum_s,
    sum_r,
    st_s,
    st_r,
    misc_s,
    misc_r,
    home_s,
    home_r,
    local_sem,
):
    seq, mp = lax.axis_index("seq"), lax.axis_index("mp")
    y, zl = seq // 8, seq % 8
    x, zh, c = mp // 4, (mp // 2) % 2, mp % 2
    z = zh * 8 + zl

    def remote(src, dst, send, recv, to):
        return pltpu.make_async_remote_copy(
            src_ref=src,
            dst_ref=dst,
            send_sem=send,
            recv_sem=recv,
            device_id=to,
            device_id_type=MESH,
        )

    z_up, z_down = device(x, y, (z + 1) % 16, c), device(x, y, (z + 15) % 16, c)
    sibling = device(x, y, z, 1 - c)
    y_up, y_down = device(x, (y + 1) % 4, z, c), device(x, (y + 3) % 4, z, c)
    plane = [device((x + i % 4) % 4, (y + i // 4) % 4, z, c) for i in range(16)]
    turn = (zl + 8 - x - y) % 4
    one_to = [device(y, turn, z, h) for h in range(2)]
    one_from = [device(turn, x, z, h) for h in range(2)]
    two_to = [device(x, y, zh * 8 + 2 * turn + h, c) for h in range(2)]
    first = (zl // 2 + x + y) % 4
    two_from = [device(x, y, zh * 8 + first + 4 * h, c) for h in range(2)]
    home_z = zh * 8 + 2 * x
    home_to = [device(zl // 2, y, home_z + q, zl % 2) for q in range(2)]
    home_from = [device(zl // 2, y, home_z + c, h) for h in range(2)]
    partner = device(zl // 2, y, home_z + c, zl % 2)
    at_home = zl == 2 * x + c
    away = jnp.logical_not(at_home)
    one_same = jnp.logical_and(x == y, turn == y)

    barrier = pltpu.get_barrier_semaphore()
    met = [z_up, z_down, sibling] + plane[1:] + one_to + one_from + two_to + two_from
    met = met + home_to + home_from
    for other in met:
        pl.semaphore_signal(barrier, inc=1, device_id=other, device_id_type=MESH)
    pl.semaphore_wait(barrier, len(met))

    def one_copy(h):
        return remote(w_ref.at[h], stage_buf.at[c], one_s.at[h], one_r.at[c], one_to[h])

    for h in range(2):
        stays = jnp.logical_and(one_same, c == h)

        @pl.when(stays)
        def _():
            stage_buf[h] = w_ref[h]

        @pl.when(jnp.logical_not(stays))
        def _():
            one_copy(h).start()

    def wait_one():
        for h in range(2):

            @pl.when(jnp.logical_not(jnp.logical_and(one_same, c == h)))
            def _():
                remote(w_ref.at[h], stage_buf.at[h], one_s.at[h], one_r.at[h], one_to[h]).wait_recv()

    rows = 128 // SUBS

    def ring_copy(way, t, u):
        held = (z + 16 - t) % 16 if way == 0 else (z + t) % 16
        dst = a_buf.at[held, c, pl.ds(u * rows, rows)]
        src = tok_ref.at[pl.ds(u * rows, rows)] if t == 0 else dst
        return remote(
            src, dst, ring_s.at[way, t, u], ring_r.at[way, t, u], z_up if way == 0 else z_down
        )

    def sib_copy(way, t, u):
        held = (z + 16 - t) % 16 if way == 0 else (z + t) % 16
        dst = a_buf.at[held, c, pl.ds(u * rows, rows)]
        src = tok_ref.at[pl.ds(u * rows, rows)] if t == 0 else dst
        return remote(src, dst, sib_s.at[way, t, u], sib_r.at[way, t, u], sibling)

    def uses(way, t):
        if t < 7:
            return range(SUBS)
        return range(SUBS // 2) if way == 0 else range(SUBS // 2, SUBS)

    ring_sent, sib_sent = [], []
    for u in range(SUBS):
        for way in range(2):
            copy = ring_copy(way, 0, u)
            copy.start()
            ring_sent.append(copy)
    for u in range(SUBS):
        copy = sib_copy(0, 0, u)
        copy.start()
        sib_sent.append(copy)
    a_buf[z, c] = tok_ref[...]

    prm_copy = remote(prm_ref.at[zl % 2], prm_buf, misc_s.at[0], misc_r.at[0], partner)

    @pl.when(at_home)
    def _():
        prm_buf[...] = prm_ref[zl % 2]

    @pl.when(away)
    def _():
        prm_copy.start()

    def block(index):
        return w_buf.at[pl.ds(pl.multiple_of(index * 256, 256), 256)]

    def two_copy(h):
        return remote(stage_buf.at[h], block(zl), two_s.at[h], two_r.at[zl // 4], two_to[h])

    def two_stays(h):
        return zl == 2 * turn + h

    def send_two():
        for h in range(2):

            @pl.when(two_stays(h))
            def _():
                w_buf[pl.ds(pl.multiple_of(zl * 256, 256), 256), :] = stage_buf[h]

            @pl.when(jnp.logical_not(two_stays(h)))
            def _():
                two_copy(h).start()

    def wait_two():
        for h in range(2):

            @pl.when(zl != first + 4 * h)
            def _():
                remote(
                    stage_buf.at[h], block(first + 4 * h), two_s.at[h], two_r.at[h], two_to[h]
                ).wait_recv()

    def col_copy(way, hop, h):
        step = hop if way == 0 else -hop
        ref = block((first + 4 - step) % 4 + 4 * h)
        return remote(
            ref, ref, col_s.at[way, hop, h], col_r.at[way, hop, h], y_up if way == 0 else y_down
        )

    col_sent = []

    def spread():
        for h in range(2):
            for way in range(2):
                copy = col_copy(way, 0, h)
                copy.start()
                col_sent.append(copy)

    def forward():
        for way in range(2):
            col_copy(way, 0, way).wait_recv()
            copy = col_copy(way, 1, way)
            copy.start()
            col_sent.append(copy)

    for t in range(1, 9):
        for u in range(SUBS):
            for way in range(2):
                if u in uses(way, t - 1):
                    ring_copy(way, t - 1, u).wait_recv()
                    if t < 8 and u in uses(way, t):
                        copy = ring_copy(way, t, u)
                        copy.start()
                        ring_sent.append(copy)
                    copy = sib_copy(way, t, u)
                    copy.start()
                    sib_sent.append(copy)
        if t == STAGE_TWO:
            wait_one()
            send_two()
        if t == SPREAD:
            wait_two()
            spread()
        if t == FORWARD:
            forward()
    for way in range(2):
        col_copy(way, 0, 1 - way).wait_recv()
        col_copy(way, 1, way).wait_recv()
    for copy in sib_sent:
        copy.wait_recv()

    def sum_copy(k, r):
        to = r // 2
        return remote(
            part_buf.at[r],
            sum_buf.at[(x + 4 - to) % 4, r % 2],
            sum_s.at[k],
            sum_r.at[(x + 4 - to) % 4, r % 2],
            device(to, y, z, c),
        )

    def product(k, r):
        total = jnp.zeros((128, 384), jnp.float32)
        for half in range(2):
            for core in range(2):
                at = (half * 4 + core * 2) * 256
                total += jnp.dot(
                    a_buf[half * 8 + r, core],
                    w_buf[at : at + 512, :],
                    preferred_element_type=jnp.float32,
                )
        part_buf[r] = total.astype(jnp.bfloat16)

    def row_of(k):
        return (2 * x + 2 + k) % 8

    @pl.loop(0, 6)
    def _(k):
        r = row_of(k)
        product(k, r)
        sum_copy(k, r).start()

    @pl.loop(6, 8)
    def _(k):
        product(k, row_of(k))

    @pl.when(away)
    def _():
        prm_copy.wait_recv()

    groups = prm_buf[16:17, :]
    rates = jnp.zeros((16, 128), jnp.float32)
    res = jnp.zeros((16, 128), jnp.float32)
    for g in range(16):
        here = groups == float(g)
        rates = jnp.where(here, modes_ref[0:16, g : g + 1], rates)
        res = jnp.where(here, modes_ref[16:32, g : g + 1], res)
    decay = jnp.exp(-rates)
    decay_64 = jnp.exp(-64.0 * rates)
    decay_256 = jnp.exp(-256.0 * rates)

    for q in range(2):
        total = part_buf[2 * x + q].astype(jnp.float32)
        for i in range(1, 4):
            remote(
                part_buf.at[0], sum_buf.at[i, q], sum_s.at[0], sum_r.at[i, q], plane[1]
            ).wait_recv()
            total += sum_buf[i, q].astype(jnp.float32)
        rounded = total.astype(jnp.bfloat16)
        ext_buf[8 + 128 * q : 136 + 128 * q, :] = rounded.astype(jnp.float32)
        if q == 1:
            halo_send[...] = rounded[112:128, :]
    halo_copy = remote(
        halo_send,
        halo_recv,
        misc_s.at[1],
        misc_r.at[1],
        device((x + 1) % 4, (y + (x + 1) // 4) % 4, z, c),
    )
    halo_copy.start()
    halo_copy.wait_recv()
    is_first = jnp.logical_and(x == 0, y == 0)
    for i in range(2):
        for b in range(3):
            lanes = slice(128 * b, 128 * b + 128)
            row = halo_recv[:, lanes].astype(jnp.float32)[14 + i : 15 + i, :]
            carried = prm_buf[9 + 3 * i + b : 10 + 3 * i + b, :]
            ext_buf[6 + i : 7 + i, lanes] = jnp.where(is_first, carried, row)

    def mixed(b):
        lanes = slice(128 * b, 128 * b + 128)
        return (
            prm_buf[b : b + 1, :] * ext_buf[8:264, lanes]
            + prm_buf[3 + b : 4 + b, :] * ext_buf[7:263, lanes]
            + prm_buf[6 + b : 7 + b, :] * ext_buf[6:262, lanes]
        )

    query_buf[...] = mixed(0)
    gated_buf[...] = (mixed(1) * mixed(2)).astype(jnp.bfloat16).astype(jnp.float32)

    def leave(i, sums):
        return tuple(
            decay * s + jnp.broadcast_to(gated_buf[pl.ds(64 * k + i, 1), :], (16, 128))
            for k, s in enumerate(sums)
        )

    zero = jnp.zeros((16, 128), jnp.float32)
    sums = lax.fori_loop(0, 64, leave, (zero,) * 4)
    mine = 4 * y + x
    state_buf[mine] = sums[3] + decay_64 * (
        sums[2] + decay_64 * (sums[1] + decay_64 * sums[0])
    )

    def state_copy(i):
        return remote(
            state_buf.at[mine], state_buf.at[mine], st_s.at[i], st_r.at[i], plane[i]
        )

    for i in range(1, 16):
        state_copy(i).start()
    for i in range(1, 16):
        state_copy(i).wait_recv()
    state = prm_buf[24:40, :]
    for m in range(15):
        state = jnp.where(m < mine, decay_256 * state + state_buf[m], state)
    states = [state]
    for k in range(3):
        states.append(decay_64 * states[-1] + sums[k])

    def advance(i, held):
        new = []
        for k, s in enumerate(held):
            at = pl.ds(64 * k + i, 1)
            s = decay * s + jnp.broadcast_to(gated_buf[at, :], (16, 128))
            long_buf[at, :] = jnp.sum(res * s, axis=0, keepdims=True)
            new.append(s)
        return tuple(new)

    lax.fori_loop(0, 64, advance, tuple(states))

    long_rows = long_buf[...].astype(jnp.bfloat16).astype(jnp.float32)
    result = query_buf[...] * (long_rows + prm_buf[15:16, :] * gated_buf[...])
    result = result.astype(jnp.bfloat16)
    home_send[0] = result[0:128, :]
    home_send[1] = result[128:256, :]

    def home_copy(q):
        return remote(home_send.at[q], home_recv.at[c], home_s.at[q], home_r.at[c], home_to[q])

    for q in range(2):
        stays = jnp.logical_and(at_home, c == q)

        @pl.when(stays)
        def _():
            home_recv[q] = home_send[q]

        @pl.when(jnp.logical_not(stays))
        def _():
            home_copy(q).start()

    for copy in ring_sent + sib_sent + col_sent:
        copy.wait_send()
    for h in range(2):

        @pl.when(jnp.logical_not(jnp.logical_and(one_same, c == h)))
        def _():
            one_copy(h).wait_send()

        @pl.when(jnp.logical_not(two_stays(h)))
        def _():
            two_copy(h).wait_send()

    @pl.when(away)
    def _():
        prm_copy.wait_send()

    @pl.loop(0, 6)
    def _(k):
        sum_copy(k, row_of(k)).wait_send()

    halo_copy.wait_send()
    for i in range(1, 16):
        state_copy(i).wait_send()
    for q in range(2):

        @pl.when(jnp.logical_not(jnp.logical_and(at_home, c == q)))
        def _():
            home_copy(q).wait_send()
            remote(
                home_send.at[q], home_recv.at[q], home_s.at[q], home_r.at[q], home_to[q]
            ).wait_recv()

    for h in range(2):
        out_ref[:, 128 * h : 128 * h + 128] = home_recv[h]


def shards(
    tokens, in_weight, short_taps, carry_rows, pole_rates, residues, carry_state, skip_gain, groups
):
    depth = in_weight.shape[0]
    weight = in_weight.reshape(depth, 3, 2, 128).transpose(2, 0, 1, 3).reshape(2, depth, 384)
    width = skip_gain.shape[0]
    packed = jnp.concatenate(
        [
            short_taps.reshape(9, width),
            carry_rows.astype(jnp.float32).reshape(6, width),
            skip_gain[None],
            groups.astype(jnp.float32)[None],
            jnp.zeros((7, width), jnp.float32),
            carry_state.T,
        ],
        axis=0,
    )
    packed = packed.reshape(40, 2, 128).transpose(1, 0, 2)
    modes = jnp.concatenate([pole_rates.T, residues.T], axis=0)
    vmem = pl.BlockSpec(memory_space=pltpu.VMEM)
    dma = pltpu.SemaphoreType.DMA
    return pl.pallas_call(
        kernel,
        out_shape=jax.ShapeDtypeStruct((128, 256), jnp.bfloat16),
        in_specs=[vmem] * 4,
        out_specs=vmem,
        scratch_shapes=[
            pltpu.VMEM((16, 2, 128, 512), jnp.bfloat16),
            pltpu.VMEM((2, 256, 384), jnp.bfloat16),
            pltpu.VMEM((2048, 384), jnp.bfloat16),
            pltpu.VMEM((8, 128, 384), jnp.bfloat16),
            pltpu.VMEM((4, 2, 128, 384), jnp.bfloat16),
            pltpu.VMEM((40, 128), jnp.float32),
            pltpu.VMEM((264, 384), jnp.float32),
            pltpu.VMEM((256, 128), jnp.float32),
            pltpu.VMEM((256, 128), jnp.float32),
            pltpu.VMEM((256, 128), jnp.float32),
            pltpu.VMEM((16, 16, 128), jnp.float32),
            pltpu.VMEM((16, 384), jnp.bfloat16),
            pltpu.VMEM((16, 384), jnp.bfloat16),
            pltpu.VMEM((2, 128, 128), jnp.bfloat16),
            pltpu.VMEM((2, 128, 128), jnp.bfloat16),
            dma((2, 8, SUBS)),
            dma((2, 8, SUBS)),
            dma((2, 9, SUBS)),
            dma((2, 9, SUBS)),
            dma((2,)),
            dma((2,)),
            dma((2,)),
            dma((2,)),
            dma((2, 2, 2)),
            dma((2, 2, 2)),
            dma((8,)),
            dma((4, 2)),
            dma((16,)),
            dma((16,)),
            dma((2,)),
            dma((2,)),
            dma((2,)),
            dma((2,)),
            dma,
        ],
        compiler_params=pltpu.CompilerParams(
            collective_id=0, has_side_effects=True, vmem_limit_bytes=40 * 1024 * 1024
        ),
        name="operator",
    )(tokens, weight, packed, modes)


def solution(mesh):
    in_specs = (
        P("seq", "mp"),
        P("seq", None, "mp"),
        P(None, None, "mp"),
        P(None, None, "mp"),
        P(),
        P(),
        P("mp", None),
        P("mp"),
        P("mp"),
    )
    out_specs = P("seq", "mp")
    return jax.shard_map(shards, mesh=mesh, in_specs=in_specs, out_specs=out_specs, check_vma=False)
```

```python
import jax
import jax.numpy as jnp
from jax import lax
from jax.experimental import pallas as pl
from jax.experimental.pallas import tpu as pltpu
from jax.sharding import PartitionSpec as P

MESH = pl.DeviceIdType.MESH
SUBS = 4
MOVE, SPREAD, FORWARD = (2, 8), (4, 9), (6, 10)
BRANCHES = ((1, 2), (0, 1))


def device(x, y, z, c):
    return {"seq": y * 8 + z % 8, "mp": x * 4 + (z // 8) * 2 + c}


def kernel(
    tok_in,
    w_in,
    taps_in,
    carry_in,
    pole_in,
    res_in,
    start_in,
    skip_in,
    group_in,
    out_ref,
    tok_ref,
    w_ref,
    taps_ref,
    carry_ref,
    pole_ref,
    res_ref,
    start_ref,
    skip_ref,
    group_ref,
    a_buf,
    stage_buf,
    w_buf,
    part_kv,
    part_q,
    sum_kv,
    sum_q,
    prm_send,
    prm_buf,
    turn_buf,
    mode_buf,
    ext_buf,
    gated_buf,
    long_buf,
    state_buf,
    halo_send,
    halo_recv,
    home_send,
    home_recv,
    ring_s,
    ring_r,
    sib_s,
    sib_r,
    one_s,
    one_r,
    two_s,
    two_r,
    col_s,
    col_r,
    sum_s,
    sum_r,
    st_s,
    st_r,
    prm_s,
    prm_r,
    halo_s,
    halo_r,
    home_s,
    home_r,
    in_s,
):
    taken = [
        pltpu.make_async_copy(src, dst, in_s.at[i])
        for i, (src, dst) in enumerate(
            (
                (tok_in, tok_ref),
                (w_in, w_ref),
                (taps_in, taps_ref),
                (carry_in, carry_ref),
                (pole_in, pole_ref),
                (res_in, res_ref),
                (start_in, start_ref),
                (skip_in, skip_ref),
                (group_in, group_ref),
            )
        )
    ]
    for copy in taken:
        copy.start()
    seq, mp = lax.axis_index("seq"), lax.axis_index("mp")
    y, zl = seq // 8, seq % 8
    x, zh, c = mp // 4, (mp // 2) % 2, mp % 2
    z = zh * 8 + zl

    def remote(src, dst, send, recv, to):
        return pltpu.make_async_remote_copy(
            src_ref=src,
            dst_ref=dst,
            send_sem=send,
            recv_sem=recv,
            device_id=to,
            device_id_type=MESH,
        )

    z_up, z_down = device(x, y, (z + 1) % 16, c), device(x, y, (z + 15) % 16, c)
    sibling = device(x, y, z, 1 - c)
    y_up, y_down = device(x, (y + 1) % 4, z, c), device(x, (y + 3) % 4, z, c)
    plane = [device((x + i % 4) % 4, (y + i // 4) % 4, z, c) for i in range(16)]
    turn = (zl + 8 - x - y) % 4
    one_to = [device(y, turn, z, h) for h in range(2)]
    one_from = [device(turn, x, z, h) for h in range(2)]
    two_to = [device(x, y, zh * 8 + 2 * turn + h, c) for h in range(2)]
    first = (zl // 2 + x + y) % 4
    two_from = [device(x, y, zh * 8 + first + 4 * h, c) for h in range(2)]
    own = (x + zl // 2) % 4
    home_to = [device(zl // 2, y, zh * 8 + 2 * own + q, zl % 2) for q in range(2)]
    owner = (zl // 2 + 4 - x) % 4
    home_from = [device(owner, y, zh * 8 + 2 * x + c, h) for h in range(2)]
    partner = device(owner, y, zh * 8 + 2 * x + c, zl % 2)
    at_home = jnp.logical_and(zl // 2 == x, zl == 2 * own + c)
    away = jnp.logical_not(at_home)
    one_same = jnp.logical_and(x == y, turn == y)

    barrier = pltpu.get_barrier_semaphore()
    met = [z_up, z_down, sibling] + plane[1:] + one_to + one_from + two_to + two_from
    met = met + home_to + home_from
    for other in met:
        pl.semaphore_signal(barrier, inc=1, device_id=other, device_id_type=MESH)

    for copy in taken:
        copy.wait()

    def half(rows):
        return jnp.where(zl % 2 == 0, rows[:, 0:128], rows[:, 128:256])

    for tap in range(3):
        prm_send[3 * tap : 3 * tap + 3, :] = half(taps_ref[tap])
    for b in range(3):
        pair = half(carry_ref[b].astype(jnp.float32))
        for i in range(2):
            prm_send[9 + 3 * i + b : 10 + 3 * i + b, :] = pair[i : i + 1, :]
    prm_send[15:16, :] = half(skip_ref[...])
    prm_send[16:17, :] = half(group_ref[...].astype(jnp.float32))
    prm_send[17:24, :] = jnp.zeros((7, 128), jnp.float32)
    prm_send[24:40, :] = half(start_ref[...])
    turn_buf[...] = jnp.zeros((128, 128), jnp.float32)
    turn_buf[0:16, 0:16] = pole_ref[...]
    turn_buf[16:32, 0:16] = res_ref[...]
    turn_buf[...] = jnp.transpose(turn_buf[...])

    pl.semaphore_wait(barrier, len(met))

    def one_copy(h, p, landed=None):
        some = pl.ds(*BRANCHES[p])
        at = c if landed is None else landed
        src = w_ref.at[some, :, pl.ds(h * 128, 128)]
        return remote(src, stage_buf.at[at, some], one_s.at[h, p], one_r.at[at, p], one_to[h])

    def one_stays(h):
        return jnp.logical_and(one_same, c == h)

    def set_out(p):
        for h in range(2):

            @pl.when(jnp.logical_not(one_stays(h)))
            def _():
                one_copy(h, p).start()

    set_out(0)

    rows = 128 // SUBS

    def held(way, t):
        return (z + 16 - t) % 16 if way == 0 else (z + t) % 16

    def ring_copy(way, t, u):
        part = pl.ds(u * rows, rows)
        dst = a_buf.at[held(way, t), c, part]
        src = tok_ref.at[part] if t == 0 else dst
        to = z_up if way == 0 else z_down
        return remote(src, dst, ring_s.at[way, t, u], ring_r.at[way, t, u], to)

    def sib_copy(way, t):
        part = pl.ds(0, 128) if t < 8 else pl.ds(64 * way, 64)
        dst = a_buf.at[held(way, t), c, part]
        src = tok_ref if t == 0 else dst
        return remote(src, dst, sib_s.at[way, t], sib_r.at[way, t], sibling)

    def uses(way, t):
        if t < 7:
            return range(SUBS)
        return range(SUBS // 2) if way == 0 else range(SUBS // 2, SUBS)

    sent, sib_sent = [], []
    for u in range(SUBS):
        for way in range(2):
            copy = ring_copy(way, 0, u)
            copy.start()
            sent.append(copy)
    copy = sib_copy(0, 0)
    copy.start()
    sib_sent.append(copy)

    prm_copy = remote(prm_send, prm_buf, prm_s.at[0], prm_r.at[0], partner)

    @pl.when(away)
    def _():
        prm_copy.start()

    @pl.when(at_home)
    def _():
        prm_buf[...] = prm_send[...]

    a_buf[z, c] = tok_ref[...]
    for h in range(2):

        @pl.when(one_stays(h))
        def _():
            stage_buf[h] = w_ref[:, :, h * 128 : h * 128 + 128]

    def block(index, p):
        at = pl.ds(pl.multiple_of(index * 256, 256), 256)
        return w_buf.at[pl.ds(*BRANCHES[p]), at]

    def two_copy(h, p):
        src = stage_buf.at[h, pl.ds(*BRANCHES[p])]
        return remote(src, block(zl, p), two_s.at[h, p], two_r.at[zl // 4, p], two_to[h])

    def two_stays(h):
        return zl == 2 * turn + h

    def move(h, p):
        @pl.when(jnp.logical_not(one_stays(h)))
        def _():
            one_copy(h, p, h).wait_recv()

        @pl.when(two_stays(h))
        def _():
            low, count = BRANCHES[p]
            at = pl.ds(pl.multiple_of(zl * 256, 256), 256)
            for b in range(low, low + count):
                w_buf[b, at, :] = stage_buf[h, b]

        @pl.when(jnp.logical_not(two_stays(h)))
        def _():
            two_copy(h, p).start()

    def col_copy(way, hop, h, p):
        step = hop if way == 0 else -hop
        ref = block((first + 4 - step) % 4 + 4 * h, p)
        to = y_up if way == 0 else y_down
        return remote(ref, ref, col_s.at[way, hop, h, p], col_r.at[way, hop, h, p], to)

    def spread(h, p):
        @pl.when(zl != first + 4 * h)
        def _():
            src = stage_buf.at[h, pl.ds(*BRANCHES[p])]
            dst = block(first + 4 * h, p)
            remote(src, dst, two_s.at[h, p], two_r.at[h, p], two_to[h]).wait_recv()

        for way in range(2):
            copy = col_copy(way, 0, h, p)
            copy.start()
            sent.append(copy)

    def forward(way, p):
        col_copy(way, 0, way, p).wait_recv()
        copy = col_copy(way, 1, way, p)
        copy.start()
        sent.append(copy)

    def gathered(p):
        for way in range(2):
            col_copy(way, 0, 1 - way, p).wait_recv()
            col_copy(way, 1, way, p).wait_recv()

    def weights_at(t):
        for p in range(2):
            for h in range(2):
                if t == MOVE[p]:
                    move(h, p)
            if t == MOVE[0] and p == 0:
                set_out(1)
            for h in range(2):
                if t == SPREAD[p]:
                    spread(h, p)
            for h in range(2):
                if t == FORWARD[p]:
                    forward(h, p)

    def modes():
        @pl.when(away)
        def _():
            prm_copy.wait_recv()

        groups = prm_buf[16:17, :]
        rates = jnp.zeros((16, 128), jnp.float32)
        res = jnp.zeros((16, 128), jnp.float32)
        for g in range(16):
            here = groups == float(g)
            rates = jnp.where(here, turn_buf[0:16, g : g + 1], rates)
            res = jnp.where(here, turn_buf[0:16, 16 + g : 17 + g], res)
        mode_buf[0] = jnp.exp(-rates)
        mode_buf[1] = jnp.exp(-64.0 * rates)
        mode_buf[2] = jnp.exp(-256.0 * rates)
        mode_buf[3] = res

    for t in range(1, 9):
        for u in range(SUBS):
            for way in range(2):
                if u in uses(way, t - 1):
                    ring_copy(way, t - 1, u).wait_recv()
                    if t < 8 and u in uses(way, t):
                        copy = ring_copy(way, t, u)
                        copy.start()
                        sent.append(copy)
        for way in range(2):
            copy = sib_copy(way, t)
            copy.start()
            sib_sent.append(copy)
        weights_at(t)
        if t == 5:
            modes()
    gathered(0)
    for copy in sib_sent:
        copy.wait_recv()

    def sum_copy(p, k):
        part, to_buf = ((part_kv, sum_kv), (part_q, sum_q))[p]
        to = (x + 1 + k) % 4
        return remote(
            part.at[k], to_buf.at[k], sum_s.at[p, k], sum_r.at[p, k], device(to, y, z, c)
        )

    def product(p, to):
        total = None
        for side in range(2):
            for core in range(2):
                at = slice((side * 4 + core * 2) * 256, (side * 4 + core * 2) * 256 + 512)
                left = a_buf[pl.ds(side * 8 + 2 * ((to + zl // 2) % 4), 2), core].reshape(256, 512)
                if p == 0:
                    right = jnp.concatenate([w_buf[1, at, :], w_buf[2, at, :]], axis=1)
                else:
                    right = w_buf[0, at, :]
                term = jnp.dot(left, right, preferred_element_type=jnp.float32)
                total = term if total is None else total + term
        return total

    lanes_of = (slice(128, 384), slice(0, 128))

    def products(p):
        part = (part_kv, part_q)[p]

        @pl.loop(0, 3)
        def _(k):
            part[k] = product(p, (x + 1 + k) % 4).astype(jnp.bfloat16)
            sum_copy(p, k).start()

        ext_buf[8:264, lanes_of[p]] = product(p, x)

    halo_to = device((x + 1) % 4, (y + (own + 1) // 4) % 4, z, c)
    is_first = jnp.logical_and(own == 0, y == 0)

    def halo_copy(p):
        part = pl.ds(lanes_of[p].start, lanes_of[p].stop - lanes_of[p].start)
        return remote(
            halo_send.at[:, part], halo_recv.at[:, part], halo_s.at[p], halo_r.at[p], halo_to
        )

    def collect(p):
        got = (sum_kv, sum_q)[p]
        total = ext_buf[8:264, lanes_of[p]]
        for k in range(3):
            sum_copy(p, k).wait_recv()
            total += got[k].astype(jnp.float32)
        rounded = total.astype(jnp.bfloat16)
        halo_send[:, lanes_of[p]] = rounded[240:256, :]
        halo_copy(p).start()
        ext_buf[8:264, lanes_of[p]] = rounded.astype(jnp.float32)

    def join(p):
        halo_copy(p).wait_recv()
        low, count = BRANCHES[p]
        for b in range(low, low + count):
            lanes = slice(128 * b, 128 * b + 128)
            last = halo_recv[:, lanes].astype(jnp.float32)
            for i in range(2):
                carried = prm_buf[9 + 3 * i + b : 10 + 3 * i + b, :]
                ext_buf[6 + i : 7 + i, lanes] = jnp.where(
                    is_first, carried, last[14 + i : 15 + i, :]
                )

    def mixed(b):
        lanes = slice(128 * b, 128 * b + 128)
        return (
            prm_buf[b : b + 1, :] * ext_buf[8:264, lanes]
            + prm_buf[3 + b : 4 + b, :] * ext_buf[7:263, lanes]
            + prm_buf[6 + b : 7 + b, :] * ext_buf[6:262, lanes]
        )

    products(0)
    weights_at(8 + 1)
    collect(0)
    join(0)
    gated_buf[...] = (mixed(1) * mixed(2)).astype(jnp.bfloat16).astype(jnp.float32)

    decay, decay_64, decay_256, res = [mode_buf[i] for i in range(4)]

    def leave(i, sums):
        new = []
        for k, s in enumerate(sums):
            some = gated_buf[pl.ds(pl.multiple_of(64 * k + 8 * i, 8), 8), :]
            for j in range(8):
                s = decay * s + jnp.broadcast_to(some[j : j + 1, :], (16, 128))
            new.append(s)
        return tuple(new)

    zero = jnp.zeros((16, 128), jnp.float32)
    sums = lax.fori_loop(0, 8, leave, (zero,) * 4)
    mine = 4 * y + own
    state_buf[mine] = sums[3] + decay_64 * (
        sums[2] + decay_64 * (sums[1] + decay_64 * sums[0])
    )

    def state_copy(i):
        here = state_buf.at[mine]
        return remote(here, here, st_s.at[i], st_r.at[i], plane[i])

    for i in range(1, 16):
        state_copy(i).start()

    weights_at(8 + 2)
    gathered(1)
    products(1)

    for i in range(1, 16):
        state_copy(i).wait_recv()
    state = prm_buf[24:40, :]
    for m in range(15):
        state = jnp.where(m < mine, decay_256 * state + state_buf[m], state)
    states = [state]
    for k in range(3):
        states.append(decay_64 * states[-1] + sums[k])
    collect(1)

    def advance(i, held_states):
        new = []
        for k, s in enumerate(held_states):
            at = pl.ds(pl.multiple_of(64 * k + 8 * i, 8), 8)
            some = gated_buf[at, :]
            out = []
            for j in range(8):
                s = decay * s + jnp.broadcast_to(some[j : j + 1, :], (16, 128))
                out.append(jnp.sum(res * s, axis=0, keepdims=True))
            long_buf[at, :] = jnp.concatenate(out, axis=0)
            new.append(s)
        return tuple(new)

    lax.fori_loop(0, 8, advance, tuple(states))

    join(1)
    long_rows = long_buf[...].astype(jnp.bfloat16).astype(jnp.float32)
    result = mixed(0) * (long_rows + prm_buf[15:16, :] * gated_buf[...])
    result = result.astype(jnp.bfloat16)
    home_send[0] = result[0:128, :]
    home_send[1] = result[128:256, :]

    def home_copy(q):
        return remote(home_send.at[q], home_recv.at[c], home_s.at[q], home_r.at[c], home_to[q])

    for q in range(2):
        stays = jnp.logical_and(at_home, c == q)

        @pl.when(stays)
        def _():
            home_recv[q] = home_send[q]

        @pl.when(jnp.logical_not(stays))
        def _():
            home_copy(q).start()

    for copy in sent + sib_sent:
        copy.wait_send()
    for p in range(2):
        for h in range(2):

            @pl.when(jnp.logical_not(one_stays(h)))
            def _():
                one_copy(h, p).wait_send()

            @pl.when(jnp.logical_not(two_stays(h)))
            def _():
                two_copy(h, p).wait_send()

        for k in range(3):
            sum_copy(p, k).wait_send()
        halo_copy(p).wait_send()

    @pl.when(away)
    def _():
        prm_copy.wait_send()

    for i in range(1, 16):
        state_copy(i).wait_send()
    for q in range(2):

        @pl.when(jnp.logical_not(jnp.logical_and(at_home, c == q)))
        def _():
            home_copy(q).wait_send()
            remote(
                home_send.at[q], home_recv.at[q], home_s.at[q], home_r.at[q], home_to[q]
            ).wait_recv()

    for h in range(2):
        out_ref[:, 128 * h : 128 * h + 128] = home_recv[h]


def shards(
    tokens, in_weight, short_taps, carry_rows, pole_rates, residues, carry_state, skip_gain, groups
):
    vmem = pl.BlockSpec(memory_space=pltpu.VMEM)
    dma = pltpu.SemaphoreType.DMA
    bf16, f32 = jnp.bfloat16, jnp.float32
    operands = (
        tokens,
        in_weight.transpose(1, 0, 2),
        short_taps,
        carry_rows.transpose(1, 0, 2),
        pole_rates,
        residues,
        carry_state.T,
        skip_gain[None],
        groups[None],
    )
    return pl.pallas_call(
        kernel,
        out_shape=jax.ShapeDtypeStruct((128, 256), bf16),
        in_specs=[pl.BlockSpec(memory_space=pl.ANY)] * 9,
        out_specs=vmem,
        scratch_shapes=[pltpu.VMEM(a.shape, a.dtype) for a in operands]
        + [
            pltpu.VMEM((16, 2, 128, 512), bf16),
            pltpu.VMEM((2, 3, 256, 128), bf16),
            pltpu.VMEM((3, 2048, 128), bf16),
            pltpu.VMEM((3, 256, 256), bf16),
            pltpu.VMEM((3, 256, 128), bf16),
            pltpu.VMEM((3, 256, 256), bf16),
            pltpu.VMEM((3, 256, 128), bf16),
            pltpu.VMEM((40, 128), f32),
            pltpu.VMEM((40, 128), f32),
            pltpu.VMEM((128, 128), f32),
            pltpu.VMEM((4, 16, 128), f32),
            pltpu.VMEM((264, 384), f32),
            pltpu.VMEM((256, 128), f32),
            pltpu.VMEM((256, 128), f32),
            pltpu.VMEM((16, 16, 128), f32),
            pltpu.VMEM((16, 384), bf16),
            pltpu.VMEM((16, 384), bf16),
            pltpu.VMEM((2, 128, 128), bf16),
            pltpu.VMEM((2, 128, 128), bf16),
            dma((2, 8, SUBS)),
            dma((2, 8, SUBS)),
            dma((2, 9)),
            dma((2, 9)),
            dma((2, 2)),
            dma((2, 2)),
            dma((2, 2)),
            dma((2, 2)),
            dma((2, 2, 2, 2)),
            dma((2, 2, 2, 2)),
            dma((2, 3)),
            dma((2, 3)),
            dma((16,)),
            dma((16,)),
            dma((1,)),
            dma((1,)),
            dma((2,)),
            dma((2,)),
            dma((2,)),
            dma((2,)),
            dma((9,)),
        ],
        compiler_params=pltpu.CompilerParams(
            collective_id=0, has_side_effects=True, vmem_limit_bytes=63 * 1024 * 1024
        ),
        name="operator",
    )(*operands)


def solution(mesh):
    in_specs = (
        P("seq", "mp"),
        P("seq", None, "mp"),
        P(None, None, "mp"),
        P(None, None, "mp"),
        P(),
        P(),
        P("mp", None),
        P("mp"),
        P("mp"),
    )
    out_specs = P("seq", "mp")
    return jax.shard_map(shards, mesh=mesh, in_specs=in_specs, out_specs=out_specs, check_vma=False)
```

```python
import jax
import jax.numpy as jnp
from jax import lax
from jax.experimental import pallas as pl
from jax.experimental.pallas import tpu as pltpu
from jax.sharding import PartitionSpec as P

MESH = pl.DeviceIdType.MESH
SUBS = 4
MOVE, SPREAD, FORWARD = (2, 3, 8), (4, 5, 9), (6, 7, 10)
START = (0, 0, 3)
PIECES = ((1, 1), (2, 1), (0, 1))
BRANCHES = ((1, 2), (0, 1))


def device(x, y, z, c):
    return {"seq": y * 8 + z % 8, "mp": x * 4 + (z // 8) * 2 + c}


def kernel(
    tok_in,
    w_in,
    taps_in,
    carry_in,
    pole_in,
    res_in,
    start_in,
    skip_in,
    group_in,
    out_ref,
    tok_ref,
    w_ref,
    taps_ref,
    carry_ref,
    pole_ref,
    res_ref,
    start_ref,
    skip_ref,
    group_ref,
    a_buf,
    stage_buf,
    w_buf,
    part_kv,
    part_q,
    sum_kv,
    sum_q,
    prm_send,
    prm_buf,
    turn_buf,
    mode_buf,
    ext_buf,
    gated_buf,
    long_buf,
    state_buf,
    halo_send,
    halo_recv,
    home_send,
    home_recv,
    ring_s,
    ring_r,
    sib_s,
    sib_r,
    one_s,
    one_r,
    two_s,
    two_r,
    col_s,
    col_r,
    sum_s,
    sum_r,
    st_s,
    st_r,
    prm_s,
    prm_r,
    halo_s,
    halo_r,
    home_s,
    home_r,
    in_s,
):
    taken = [
        pltpu.make_async_copy(src, dst, in_s.at[i])
        for i, (src, dst) in enumerate(
            (
                (tok_in, tok_ref),
                (w_in, w_ref),
                (taps_in, taps_ref),
                (carry_in, carry_ref),
                (pole_in, pole_ref),
                (res_in, res_ref),
                (start_in, start_ref),
                (skip_in, skip_ref),
                (group_in, group_ref),
            )
        )
    ]
    for copy in taken:
        copy.start()
    seq, mp = lax.axis_index("seq"), lax.axis_index("mp")
    y, zl = seq // 8, seq % 8
    x, zh, c = mp // 4, (mp // 2) % 2, mp % 2
    z = zh * 8 + zl

    def remote(src, dst, send, recv, to):
        return pltpu.make_async_remote_copy(
            src_ref=src,
            dst_ref=dst,
            send_sem=send,
            recv_sem=recv,
            device_id=to,
            device_id_type=MESH,
        )

    z_up, z_down = device(x, y, (z + 1) % 16, c), device(x, y, (z + 15) % 16, c)
    sibling = device(x, y, z, 1 - c)
    y_up, y_down = device(x, (y + 1) % 4, z, c), device(x, (y + 3) % 4, z, c)
    plane = [device((x + i % 4) % 4, (y + i // 4) % 4, z, c) for i in range(16)]
    turn = (zl + 8 - x - y) % 4
    one_to = [device(y, turn, z, h) for h in range(2)]
    one_from = [device(turn, x, z, h) for h in range(2)]
    two_to = [device(x, y, zh * 8 + 2 * turn + h, c) for h in range(2)]
    first = (zl // 2 + x + y) % 4
    two_from = [device(x, y, zh * 8 + first + 4 * h, c) for h in range(2)]
    own = (x + zl // 2) % 4
    home_to = [device(zl // 2, y, zh * 8 + 2 * own + q, zl % 2) for q in range(2)]
    owner = (zl // 2 + 4 - x) % 4
    home_from = [device(owner, y, zh * 8 + 2 * x + c, h) for h in range(2)]
    partner = device(owner, y, zh * 8 + 2 * x + c, zl % 2)
    at_home = jnp.logical_and(zl // 2 == x, zl == 2 * own + c)
    away = jnp.logical_not(at_home)
    one_same = jnp.logical_and(x == y, turn == y)

    barrier = pltpu.get_barrier_semaphore()
    met = [z_up, z_down, sibling] + plane[1:] + one_to + one_from + two_to + two_from
    met = met + home_to + home_from
    for other in met:
        pl.semaphore_signal(barrier, inc=1, device_id=other, device_id_type=MESH)

    for copy in taken:
        copy.wait()

    def half(rows):
        return jnp.where(zl % 2 == 0, rows[:, 0:128], rows[:, 128:256])

    for tap in range(3):
        prm_send[3 * tap : 3 * tap + 3, :] = half(taps_ref[tap])
    for b in range(3):
        pair = half(carry_ref[b].astype(jnp.float32))
        for i in range(2):
            prm_send[9 + 3 * i + b : 10 + 3 * i + b, :] = pair[i : i + 1, :]
    prm_send[15:16, :] = half(skip_ref[...])
    prm_send[16:17, :] = half(group_ref[...].astype(jnp.float32))
    prm_send[17:24, :] = jnp.zeros((7, 128), jnp.float32)
    prm_send[24:40, :] = half(start_ref[...])
    turn_buf[...] = jnp.zeros((128, 128), jnp.float32)
    turn_buf[0:16, 0:16] = pole_ref[...]
    turn_buf[16:32, 0:16] = res_ref[...]
    turn_buf[...] = jnp.transpose(turn_buf[...])

    pl.semaphore_wait(barrier, len(met))

    def one_copy(h, p, landed=None):
        some = pl.ds(*PIECES[p])
        at = c if landed is None else landed
        src = w_ref.at[some, :, pl.ds(h * 128, 128)]
        return remote(src, stage_buf.at[at, some], one_s.at[h, p], one_r.at[at, p], one_to[h])

    def one_stays(h):
        return jnp.logical_and(one_same, c == h)

    def set_out(p):
        for h in range(2):

            @pl.when(jnp.logical_not(one_stays(h)))
            def _():
                one_copy(h, p).start()

    for p in range(3):
        if START[p] == 0:
            set_out(p)

    rows = 128 // SUBS

    def held(way, t):
        return (z + 16 - t) % 16 if way == 0 else (z + t) % 16

    def ring_copy(way, t, u):
        part = pl.ds(u * rows, rows)
        dst = a_buf.at[held(way, t), c, part]
        src = tok_ref.at[part] if t == 0 else dst
        to = z_up if way == 0 else z_down
        return remote(src, dst, ring_s.at[0], ring_r.at[way, t, u], to)

    def sib_copy(way, t):
        part = pl.ds(0, 128) if t < 8 else pl.ds(64 * way, 64)
        dst = a_buf.at[held(way, t), c, part]
        src = tok_ref if t == 0 else dst
        return remote(src, dst, sib_s.at[0], sib_r.at[0], sibling)

    def uses(way, t):
        if t < 7:
            return range(SUBS)
        return range(SUBS // 2) if way == 0 else range(SUBS // 2, SUBS)

    for u in range(SUBS):
        for way in range(2):
            copy = ring_copy(way, 0, u)
            copy.start()
    sib_copy(0, 0).start()

    prm_copy = remote(prm_send, prm_buf, prm_s.at[0], prm_r.at[0], partner)

    @pl.when(away)
    def _():
        prm_copy.start()

    @pl.when(at_home)
    def _():
        prm_buf[...] = prm_send[...]

    a_buf[z, c] = tok_ref[...]
    for h in range(2):

        @pl.when(one_stays(h))
        def _():
            stage_buf[h] = w_ref[:, :, h * 128 : h * 128 + 128]

    def block(index, p):
        at = pl.ds(pl.multiple_of(index * 256, 256), 256)
        return w_buf.at[pl.ds(*PIECES[p]), at]

    def two_copy(h, p):
        src = stage_buf.at[h, pl.ds(*PIECES[p])]
        return remote(src, block(zl, p), two_s.at[h, p], two_r.at[zl // 4, p], two_to[h])

    def two_stays(h):
        return zl == 2 * turn + h

    def move(h, p):
        @pl.when(jnp.logical_not(one_stays(h)))
        def _():
            one_copy(h, p, h).wait_recv()

        @pl.when(two_stays(h))
        def _():
            low, count = PIECES[p]
            at = pl.ds(pl.multiple_of(zl * 256, 256), 256)
            for b in range(low, low + count):
                w_buf[b, at, :] = stage_buf[h, b]

        @pl.when(jnp.logical_not(two_stays(h)))
        def _():
            two_copy(h, p).start()

    def col_copy(way, hop, h, p):
        step = hop if way == 0 else -hop
        ref = block((first + 4 - step) % 4 + 4 * h, p)
        to = y_up if way == 0 else y_down
        return remote(ref, ref, col_s.at[0], col_r.at[way, hop, h, p], to)

    def spread(h, p):
        @pl.when(zl != first + 4 * h)
        def _():
            src = stage_buf.at[h, pl.ds(*PIECES[p])]
            dst = block(first + 4 * h, p)
            remote(src, dst, two_s.at[h, p], two_r.at[h, p], two_to[h]).wait_recv()

        for way in range(2):
            col_copy(way, 0, h, p).start()

    def forward(way, p):
        col_copy(way, 0, way, p).wait_recv()
        col_copy(way, 1, way, p).start()

    def gathered(p):
        for way in range(2):
            col_copy(way, 0, 1 - way, p).wait_recv()
            col_copy(way, 1, way, p).wait_recv()

    def weights_at(t):
        for p in range(3):
            for h in range(2):
                if t == MOVE[p]:
                    move(h, p)
            if t == START[p]:
                set_out(p)
            for h in range(2):
                if t == SPREAD[p]:
                    spread(h, p)
            for h in range(2):
                if t == FORWARD[p]:
                    forward(h, p)

    def modes():
        @pl.when(away)
        def _():
            prm_copy.wait_recv()

        groups = prm_buf[16:17, :]
        rates = jnp.zeros((16, 128), jnp.float32)
        res = jnp.zeros((16, 128), jnp.float32)
        for g in range(16):
            here = groups == float(g)
            rates = jnp.where(here, turn_buf[0:16, g : g + 1], rates)
            res = jnp.where(here, turn_buf[0:16, 16 + g : 17 + g], res)
        mode_buf[0] = jnp.exp(-rates)
        mode_buf[1] = jnp.exp(-64.0 * rates)
        mode_buf[2] = jnp.exp(-256.0 * rates)
        mode_buf[3] = res

    for t in range(1, 9):
        for u in range(SUBS):
            for way in range(2):
                if u in uses(way, t - 1):
                    ring_copy(way, t - 1, u).wait_recv()
                    if t < 8 and u in uses(way, t):
                        copy = ring_copy(way, t, u)
                        copy.start()
        for way in range(2):
            sib_copy(way, t).start()
        weights_at(t)
        if t == 5:
            modes()
    gathered(0)
    gathered(1)
    shards_of = a_buf.at[:, 0]
    sib_all = remote(shards_of, shards_of, sib_s.at[0], sib_r.at[0], sibling)
    sib_all.wait_recv()

    def sum_copy(p, k):
        part, to_buf = ((part_kv, sum_kv), (part_q, sum_q))[p]
        to = (x + 1 + k) % 4
        return remote(
            part.at[k], to_buf.at[k], sum_s.at[p], sum_r.at[p], device(to, y, z, c)
        )

    def product(p, to):
        total = None
        for side in range(2):
            for core in range(2):
                at = slice((side * 4 + core * 2) * 256, (side * 4 + core * 2) * 256 + 512)
                left = a_buf[pl.ds(side * 8 + 2 * ((to + zl // 2) % 4), 2), core].reshape(256, 512)
                if p == 0:
                    right = jnp.concatenate([w_buf[1, at, :], w_buf[2, at, :]], axis=1)
                else:
                    right = w_buf[0, at, :]
                term = jnp.dot(left, right, preferred_element_type=jnp.float32)
                total = term if total is None else total + term
        return total

    def sum_all(p):
        part, to_buf = ((part_kv, sum_kv), (part_q, sum_q))[p]
        return remote(part, to_buf, sum_s.at[p], sum_r.at[p], plane[1])

    lanes_of = (slice(128, 384), slice(0, 128))

    def products(p):
        part = (part_kv, part_q)[p]

        @pl.loop(0, 3)
        def _(k):
            part[k] = product(p, (x + 1 + k) % 4).astype(jnp.bfloat16)
            sum_copy(p, k).start()

        ext_buf[8:264, lanes_of[p]] = product(p, x)

    halo_to = device((x + 1) % 4, (y + (own + 1) // 4) % 4, z, c)
    is_first = jnp.logical_and(own == 0, y == 0)

    def halo_copy(p):
        part = pl.ds(lanes_of[p].start, lanes_of[p].stop - lanes_of[p].start)
        return remote(
            halo_send.at[:, part], halo_recv.at[:, part], halo_s.at[p], halo_r.at[p], halo_to
        )

    def collect(p):
        got = (sum_kv, sum_q)[p]
        total = ext_buf[8:264, lanes_of[p]]
        sum_all(p).wait_recv()
        for k in range(3):
            total += got[k].astype(jnp.float32)
        rounded = total.astype(jnp.bfloat16)
        halo_send[:, lanes_of[p]] = rounded[240:256, :]
        halo_copy(p).start()
        ext_buf[8:264, lanes_of[p]] = rounded.astype(jnp.float32)

    def join(p):
        halo_copy(p).wait_recv()
        low, count = BRANCHES[p]
        for b in range(low, low + count):
            lanes = slice(128 * b, 128 * b + 128)
            last = halo_recv[:, lanes].astype(jnp.float32)
            for i in range(2):
                carried = prm_buf[9 + 3 * i + b : 10 + 3 * i + b, :]
                ext_buf[6 + i : 7 + i, lanes] = jnp.where(
                    is_first, carried, last[14 + i : 15 + i, :]
                )

    def mixed(b):
        lanes = slice(128 * b, 128 * b + 128)
        return (
            prm_buf[b : b + 1, :] * ext_buf[8:264, lanes]
            + prm_buf[3 + b : 4 + b, :] * ext_buf[7:263, lanes]
            + prm_buf[6 + b : 7 + b, :] * ext_buf[6:262, lanes]
        )

    products(0)
    weights_at(8 + 1)
    collect(0)
    weights_at(8 + 2)
    join(0)
    gated_buf[...] = (mixed(1) * mixed(2)).astype(jnp.bfloat16).astype(jnp.float32)

    decay, decay_64, decay_256, res = [mode_buf[i] for i in range(4)]

    def leave(i, sums):
        new = []
        for k, s in enumerate(sums):
            some = gated_buf[pl.ds(pl.multiple_of(64 * k + 8 * i, 8), 8), :]
            for j in range(8):
                s = decay * s + jnp.broadcast_to(some[j : j + 1, :], (16, 128))
            new.append(s)
        return tuple(new)

    zero = jnp.zeros((16, 128), jnp.float32)
    sums = lax.fori_loop(0, 8, leave, (zero,) * 4)
    mine = 4 * y + own
    state_buf[mine] = sums[3] + decay_64 * (
        sums[2] + decay_64 * (sums[1] + decay_64 * sums[0])
    )

    def state_copy(i):
        here = state_buf.at[mine]
        return remote(here, here, st_s.at[0], st_r.at[0], plane[i])

    for i in range(1, 16):
        state_copy(i).start()

    gathered(2)
    products(1)

    others = state_buf.at[pl.ds(0, 15)]
    state_all = remote(others, others, st_s.at[0], st_r.at[0], plane[1])
    state_all.wait_recv()
    state = prm_buf[24:40, :]
    for m in range(15):
        state = jnp.where(m < mine, decay_256 * state + state_buf[m], state)
    states = [state]
    for k in range(3):
        states.append(decay_64 * states[-1] + sums[k])
    collect(1)

    def advance(i, held_states):
        new = []
        for k, s in enumerate(held_states):
            at = pl.ds(pl.multiple_of(64 * k + 8 * i, 8), 8)
            some = gated_buf[at, :]
            out = []
            for j in range(8):
                s = decay * s + jnp.broadcast_to(some[j : j + 1, :], (16, 128))
                out.append(jnp.sum(res * s, axis=0, keepdims=True))
            long_buf[at, :] = jnp.concatenate(out, axis=0)
            new.append(s)
        return tuple(new)

    lax.fori_loop(0, 8, advance, tuple(states))

    join(1)
    long_rows = long_buf[...].astype(jnp.bfloat16).astype(jnp.float32)
    result = mixed(0) * (long_rows + prm_buf[15:16, :] * gated_buf[...])
    result = result.astype(jnp.bfloat16)
    home_send[0] = result[0:128, :]
    home_send[1] = result[128:256, :]

    def home_copy(q):
        return remote(home_send.at[q], home_recv.at[c], home_s.at[q], home_r.at[c], home_to[q])

    for q in range(2):
        stays = jnp.logical_and(at_home, c == q)

        @pl.when(stays)
        def _():
            home_recv[q] = home_send[q]

        @pl.when(jnp.logical_not(stays))
        def _():
            home_copy(q).start()

    all_but_one = a_buf.at[pl.ds(0, 15), 0]
    remote(all_but_one, all_but_one, ring_s.at[0], ring_r.at[0, 0, 0], z_up).wait_send()
    sib_all.wait_send()
    col_all = w_buf.at[:, pl.ds(0, 1536)]
    remote(col_all, col_all, col_s.at[0], col_r.at[0, 0, 0, 0], y_up).wait_send()
    for p in range(3):
        for h in range(2):

            @pl.when(jnp.logical_not(one_stays(h)))
            def _():
                one_copy(h, p).wait_send()

            @pl.when(jnp.logical_not(two_stays(h)))
            def _():
                two_copy(h, p).wait_send()

    for p in range(2):
        sum_all(p).wait_send()
        halo_copy(p).wait_send()

    @pl.when(away)
    def _():
        prm_copy.wait_send()

    state_all.wait_send()
    for q in range(2):

        @pl.when(jnp.logical_not(jnp.logical_and(at_home, c == q)))
        def _():
            home_copy(q).wait_send()
            remote(
                home_send.at[q], home_recv.at[q], home_s.at[q], home_r.at[q], home_to[q]
            ).wait_recv()

    for h in range(2):
        out_ref[:, 128 * h : 128 * h + 128] = home_recv[h]


def shards(
    tokens, in_weight, short_taps, carry_rows, pole_rates, residues, carry_state, skip_gain, groups
):
    vmem = pl.BlockSpec(memory_space=pltpu.VMEM)
    dma = pltpu.SemaphoreType.DMA
    bf16, f32 = jnp.bfloat16, jnp.float32
    operands = (
        tokens,
        in_weight.transpose(1, 0, 2),
        short_taps,
        carry_rows.transpose(1, 0, 2),
        pole_rates,
        residues,
        carry_state.T,
        skip_gain[None],
        groups[None],
    )
    return pl.pallas_call(
        kernel,
        out_shape=jax.ShapeDtypeStruct((128, 256), bf16),
        in_specs=[pl.BlockSpec(memory_space=pl.ANY)] * 9,
        out_specs=vmem,
        scratch_shapes=[pltpu.VMEM(a.shape, a.dtype) for a in operands]
        + [
            pltpu.VMEM((16, 2, 128, 512), bf16),
            pltpu.VMEM((2, 3, 256, 128), bf16),
            pltpu.VMEM((3, 2048, 128), bf16),
            pltpu.VMEM((3, 256, 256), bf16),
            pltpu.VMEM((3, 256, 128), bf16),
            pltpu.VMEM((3, 256, 256), bf16),
            pltpu.VMEM((3, 256, 128), bf16),
            pltpu.VMEM((40, 128), f32),
            pltpu.VMEM((40, 128), f32),
            pltpu.VMEM((128, 128), f32),
            pltpu.VMEM((4, 16, 128), f32),
            pltpu.VMEM((264, 384), f32),
            pltpu.VMEM((256, 128), f32),
            pltpu.VMEM((256, 128), f32),
            pltpu.VMEM((16, 16, 128), f32),
            pltpu.VMEM((16, 384), bf16),
            pltpu.VMEM((16, 384), bf16),
            pltpu.VMEM((2, 128, 128), bf16),
            pltpu.VMEM((2, 128, 128), bf16),
            dma((1,)),
            dma((2, 8, SUBS)),
            dma((1,)),
            dma((1,)),
            dma((2, 3)),
            dma((2, 3)),
            dma((2, 3)),
            dma((2, 3)),
            dma((1,)),
            dma((2, 2, 2, 3)),
            dma((2,)),
            dma((2,)),
            dma((1,)),
            dma((1,)),
            dma((1,)),
            dma((1,)),
            dma((2,)),
            dma((2,)),
            dma((2,)),
            dma((2,)),
            dma((9,)),
        ],
        compiler_params=pltpu.CompilerParams(
            collective_id=0, has_side_effects=True, vmem_limit_bytes=63 * 1024 * 1024
        ),
        name="operator",
    )(*operands)


def solution(mesh):
    in_specs = (
        P("seq", "mp"),
        P("seq", None, "mp"),
        P(None, None, "mp"),
        P(None, None, "mp"),
        P(),
        P(),
        P("mp", None),
        P("mp"),
        P("mp"),
    )
    out_specs = P("seq", "mp")
    return jax.shard_map(shards, mesh=mesh, in_specs=in_specs, out_specs=out_specs, check_vma=False)
```

```python
import jax
import jax.numpy as jnp
from jax import lax
from jax.experimental import pallas as pl
from jax.experimental.pallas import tpu as pltpu
from jax.sharding import PartitionSpec as P

MESH = pl.DeviceIdType.MESH
SUBS = 4
MOVE, SPREAD, FORWARD = (2, 3, 8), (4, 5, 9), (6, 7, 10)
START = (0, 0, 3)
PIECES = ((1, 1), (2, 1), (0, 1))
BRANCHES = ((1, 2), (0, 1))


def offset(pair):
    return pair // 2 * (pair - 2) + (1 - pair // 2) * (3 - pair)


def device(x, y, z, c):
    return {"seq": y * 8 + z % 8, "mp": x * 4 + (z // 8) * 2 + c}


def kernel(
    tok_in,
    w_in,
    taps_in,
    carry_in,
    pole_in,
    res_in,
    start_in,
    skip_in,
    group_in,
    out_ref,
    tok_ref,
    w_ref,
    taps_ref,
    carry_ref,
    pole_ref,
    res_ref,
    start_ref,
    skip_ref,
    group_ref,
    a_buf,
    stage_buf,
    w_buf,
    part_kv,
    part_q,
    sum_kv,
    sum_q,
    prm_send,
    prm_buf,
    turn_buf,
    mode_buf,
    ext_buf,
    gated_buf,
    long_buf,
    state_buf,
    halo_send,
    halo_recv,
    home_send,
    home_recv,
    ring_s,
    ring_r,
    sib_s,
    sib_r,
    one_s,
    one_r,
    two_s,
    two_r,
    col_s,
    col_r,
    sum_s,
    sum_r,
    st_s,
    st_r,
    prm_s,
    prm_r,
    halo_s,
    halo_r,
    home_s,
    home_r,
    in_s,
):
    taken = [
        pltpu.make_async_copy(src, dst, in_s.at[i])
        for i, (src, dst) in enumerate(
            (
                (tok_in, tok_ref),
                (w_in, w_ref),
                (taps_in, taps_ref),
                (carry_in, carry_ref),
                (pole_in, pole_ref),
                (res_in, res_ref),
                (start_in, start_ref),
                (skip_in, skip_ref),
                (group_in, group_ref),
            )
        )
    ]
    for copy in taken:
        copy.start()
    seq, mp = lax.axis_index("seq"), lax.axis_index("mp")
    y, zl = seq // 8, seq % 8
    x, zh, c = mp // 4, (mp // 2) % 2, mp % 2
    z = zh * 8 + zl

    def remote(src, dst, send, recv, to):
        return pltpu.make_async_remote_copy(
            src_ref=src,
            dst_ref=dst,
            send_sem=send,
            recv_sem=recv,
            device_id=to,
            device_id_type=MESH,
        )

    z_up, z_down = device(x, y, (z + 1) % 16, c), device(x, y, (z + 15) % 16, c)
    sibling = device(x, y, z, 1 - c)
    y_up, y_down = device(x, (y + 1) % 4, z, c), device(x, (y + 3) % 4, z, c)
    plane = [device((x + i % 4) % 4, (y + i // 4) % 4, z, c) for i in range(16)]
    turn = (zl + 8 - x - y) % 4
    one_to = [device(y, turn, z, h) for h in range(2)]
    one_from = [device(turn, x, z, h) for h in range(2)]
    two_to = [device(x, y, zh * 8 + 2 * turn + h, c) for h in range(2)]
    first = (zl // 2 + x + y) % 4
    two_from = [device(x, y, zh * 8 + first + 4 * h, c) for h in range(2)]
    own = (x + offset(zl // 2)) % 4
    home_to = [device(zl // 2, y, zh * 8 + 2 * own + q, zl % 2) for q in range(2)]
    owner = (zl // 2 + 4 - offset(x)) % 4
    home_from = [device(owner, y, zh * 8 + 2 * x + c, h) for h in range(2)]
    partner = device(owner, y, zh * 8 + 2 * x + c, zl % 2)
    at_home = jnp.logical_and(zl // 2 == x, zl == 2 * own + c)
    away = jnp.logical_not(at_home)
    one_same = jnp.logical_and(x == y, turn == y)

    barrier = pltpu.get_barrier_semaphore()
    met = [z_up, z_down, sibling] + plane[1:] + one_to + one_from + two_to + two_from
    met = met + home_to + home_from
    for other in met:
        pl.semaphore_signal(barrier, inc=1, device_id=other, device_id_type=MESH)

    for copy in taken:
        copy.wait()

    def half(rows):
        return jnp.where(zl % 2 == 0, rows[:, 0:128], rows[:, 128:256])

    for tap in range(3):
        prm_send[3 * tap : 3 * tap + 3, :] = half(taps_ref[tap])
    for b in range(3):
        pair = half(carry_ref[b].astype(jnp.float32))
        for i in range(2):
            prm_send[9 + 3 * i + b : 10 + 3 * i + b, :] = pair[i : i + 1, :]
    prm_send[15:16, :] = half(skip_ref[...])
    prm_send[16:17, :] = half(group_ref[...].astype(jnp.float32))
    prm_send[17:24, :] = jnp.zeros((7, 128), jnp.float32)
    prm_send[24:40, :] = half(start_ref[...])
    turn_buf[...] = jnp.zeros((128, 128), jnp.float32)
    turn_buf[0:16, 0:16] = pole_ref[...]
    turn_buf[16:32, 0:16] = res_ref[...]
    turn_buf[...] = jnp.transpose(turn_buf[...])

    pl.semaphore_wait(barrier, len(met))

    def one_copy(h, p, landed=None):
        some = pl.ds(*PIECES[p])
        at = c if landed is None else landed
        src = w_ref.at[some, :, pl.ds(h * 128, 128)]
        return remote(src, stage_buf.at[at, some], one_s.at[h, p], one_r.at[at, p], one_to[h])

    def one_stays(h):
        return jnp.logical_and(one_same, c == h)

    def set_out(p):
        for h in range(2):

            @pl.when(jnp.logical_not(one_stays(h)))
            def _():
                one_copy(h, p).start()

    for p in range(3):
        if START[p] == 0:
            set_out(p)

    rows = 128 // SUBS

    def held(way, t):
        return (z + 16 - t) % 16 if way == 0 else (z + t) % 16

    def ring_copy(way, t, u):
        part = pl.ds(u * rows, rows)
        dst = a_buf.at[held(way, t), c, part]
        src = tok_ref.at[part] if t == 0 else dst
        to = z_up if way == 0 else z_down
        return remote(src, dst, ring_s.at[0], ring_r.at[way, t, u], to)

    def sib_copy(way, t):
        part = pl.ds(0, 128) if t < 8 else pl.ds(64 * way, 64)
        dst = a_buf.at[held(way, t), c, part]
        src = tok_ref if t == 0 else dst
        return remote(src, dst, sib_s.at[0], sib_r.at[0], sibling)

    def uses(way, t):
        if t < 7:
            return range(SUBS)
        return range(SUBS // 2) if way == 0 else range(SUBS // 2, SUBS)

    for u in range(SUBS):
        for way in range(2):
            copy = ring_copy(way, 0, u)
            copy.start()
    sib_copy(0, 0).start()

    prm_copy = remote(prm_send, prm_buf, prm_s.at[0], prm_r.at[0], partner)

    @pl.when(away)
    def _():
        prm_copy.start()

    @pl.when(at_home)
    def _():
        prm_buf[...] = prm_send[...]

    a_buf[z, c] = tok_ref[...]
    for h in range(2):

        @pl.when(one_stays(h))
        def _():
            stage_buf[h] = w_ref[:, :, h * 128 : h * 128 + 128]

    def block(index, p):
        at = pl.ds(pl.multiple_of(index * 256, 256), 256)
        return w_buf.at[pl.ds(*PIECES[p]), at]

    def two_copy(h, p):
        src = stage_buf.at[h, pl.ds(*PIECES[p])]
        return remote(src, block(zl, p), two_s.at[h, p], two_r.at[zl // 4, p], two_to[h])

    def two_stays(h):
        return zl == 2 * turn + h

    def move(h, p):
        @pl.when(jnp.logical_not(one_stays(h)))
        def _():
            one_copy(h, p, h).wait_recv()

        @pl.when(two_stays(h))
        def _():
            low, count = PIECES[p]
            at = pl.ds(pl.multiple_of(zl * 256, 256), 256)
            for b in range(low, low + count):
                w_buf[b, at, :] = stage_buf[h, b]

        @pl.when(jnp.logical_not(two_stays(h)))
        def _():
            two_copy(h, p).start()

    def col_copy(way, hop, h, p):
        step = hop if way == 0 else -hop
        ref = block((first + 4 - step) % 4 + 4 * h, p)
        to = y_up if way == 0 else y_down
        return remote(ref, ref, col_s.at[0], col_r.at[way, hop, h, p], to)

    def spread(h, p):
        @pl.when(zl != first + 4 * h)
        def _():
            src = stage_buf.at[h, pl.ds(*PIECES[p])]
            dst = block(first + 4 * h, p)
            remote(src, dst, two_s.at[h, p], two_r.at[h, p], two_to[h]).wait_recv()

        for way in range(2):
            col_copy(way, 0, h, p).start()

    def forward(way, p):
        col_copy(way, 0, way, p).wait_recv()
        col_copy(way, 1, way, p).start()

    def gathered(p):
        for way in range(2):
            col_copy(way, 0, 1 - way, p).wait_recv()
            col_copy(way, 1, way, p).wait_recv()

    def weights_at(t):
        for p in range(3):
            for h in range(2):
                if t == MOVE[p]:
                    move(h, p)
            if t == START[p]:
                set_out(p)
            for h in range(2):
                if t == SPREAD[p]:
                    spread(h, p)
            for h in range(2):
                if t == FORWARD[p]:
                    forward(h, p)

    def modes():
        @pl.when(away)
        def _():
            prm_copy.wait_recv()

        groups = prm_buf[16:17, :]
        rates = jnp.zeros((16, 128), jnp.float32)
        res = jnp.zeros((16, 128), jnp.float32)
        for g in range(16):
            here = groups == float(g)
            rates = jnp.where(here, turn_buf[0:16, g : g + 1], rates)
            res = jnp.where(here, turn_buf[0:16, 16 + g : 17 + g], res)
        mode_buf[0] = jnp.exp(-rates)
        mode_buf[1] = jnp.exp(-64.0 * rates)
        mode_buf[2] = jnp.exp(-256.0 * rates)
        mode_buf[3] = res

    for t in range(1, 9):
        for u in range(SUBS):
            for way in range(2):
                if u in uses(way, t - 1):
                    ring_copy(way, t - 1, u).wait_recv()
                    if t < 8 and u in uses(way, t):
                        copy = ring_copy(way, t, u)
                        copy.start()
        for way in range(2):
            sib_copy(way, t).start()
        weights_at(t)
        if t == 5:
            modes()
    gathered(0)
    gathered(1)
    shards_of = a_buf.at[:, 0]
    sib_all = remote(shards_of, shards_of, sib_s.at[0], sib_r.at[0], sibling)
    sib_all.wait_recv()

    def sum_copy(p, k):
        part, to_buf = ((part_kv, sum_kv), (part_q, sum_q))[p]
        to = (x + 1 + k) % 4
        return remote(
            part.at[k], to_buf.at[k], sum_s.at[p], sum_r.at[p], device(to, y, z, c)
        )

    def product(p, to):
        total = None
        for side in range(2):
            for core in range(2):
                at = slice((side * 4 + core * 2) * 256, (side * 4 + core * 2) * 256 + 512)
                left = a_buf[pl.ds(side * 8 + 2 * ((to + offset(zl // 2)) % 4), 2), core].reshape(256, 512)
                if p == 0:
                    right = jnp.concatenate([w_buf[1, at, :], w_buf[2, at, :]], axis=1)
                else:
                    right = w_buf[0, at, :]
                term = jnp.dot(left, right, preferred_element_type=jnp.float32)
                total = term if total is None else total + term
        return total

    def sum_all(p):
        part, to_buf = ((part_kv, sum_kv), (part_q, sum_q))[p]
        return remote(part, to_buf, sum_s.at[p], sum_r.at[p], plane[1])

    lanes_of = (slice(128, 384), slice(0, 128))

    def products(p):
        part = (part_kv, part_q)[p]

        @pl.loop(0, 3)
        def _(k):
            part[k] = product(p, (x + 1 + k) % 4).astype(jnp.bfloat16)
            sum_copy(p, k).start()

        ext_buf[8:264, lanes_of[p]] = product(p, x)

    halo_to = device((x + 1) % 4, (y + (own + 1) // 4) % 4, z, c)
    is_first = jnp.logical_and(own == 0, y == 0)

    def halo_copy(p):
        part = pl.ds(lanes_of[p].start, lanes_of[p].stop - lanes_of[p].start)
        return remote(
            halo_send.at[:, part], halo_recv.at[:, part], halo_s.at[p], halo_r.at[p], halo_to
        )

    def collect(p):
        got = (sum_kv, sum_q)[p]
        total = ext_buf[8:264, lanes_of[p]]
        sum_all(p).wait_recv()
        for k in range(3):
            total += got[k].astype(jnp.float32)
        rounded = total.astype(jnp.bfloat16)
        halo_send[:, lanes_of[p]] = rounded[240:256, :]
        halo_copy(p).start()
        ext_buf[8:264, lanes_of[p]] = rounded.astype(jnp.float32)

    def join(p):
        halo_copy(p).wait_recv()
        low, count = BRANCHES[p]
        for b in range(low, low + count):
            lanes = slice(128 * b, 128 * b + 128)
            last = halo_recv[:, lanes].astype(jnp.float32)
            for i in range(2):
                carried = prm_buf[9 + 3 * i + b : 10 + 3 * i + b, :]
                ext_buf[6 + i : 7 + i, lanes] = jnp.where(
                    is_first, carried, last[14 + i : 15 + i, :]
                )

    def mixed(b):
        lanes = slice(128 * b, 128 * b + 128)
        return (
            prm_buf[b : b + 1, :] * ext_buf[8:264, lanes]
            + prm_buf[3 + b : 4 + b, :] * ext_buf[7:263, lanes]
            + prm_buf[6 + b : 7 + b, :] * ext_buf[6:262, lanes]
        )

    products(0)
    weights_at(8 + 1)
    collect(0)
    weights_at(8 + 2)
    join(0)
    gated_buf[...] = (mixed(1) * mixed(2)).astype(jnp.bfloat16).astype(jnp.float32)

    decay, decay_64, decay_256, res = [mode_buf[i] for i in range(4)]

    def leave(i, sums):
        new = []
        for k, s in enumerate(sums):
            some = gated_buf[pl.ds(pl.multiple_of(64 * k + 8 * i, 8), 8), :]
            for j in range(8):
                s = decay * s + jnp.broadcast_to(some[j : j + 1, :], (16, 128))
            new.append(s)
        return tuple(new)

    zero = jnp.zeros((16, 128), jnp.float32)
    sums = lax.fori_loop(0, 8, leave, (zero,) * 4)
    mine = 4 * y + own
    state_buf[mine] = sums[3] + decay_64 * (
        sums[2] + decay_64 * (sums[1] + decay_64 * sums[0])
    )

    def state_copy(i):
        here = state_buf.at[mine]
        return remote(here, here, st_s.at[0], st_r.at[0], plane[i])

    for i in range(1, 16):
        state_copy(i).start()

    gathered(2)
    products(1)

    others = state_buf.at[pl.ds(0, 15)]
    state_all = remote(others, others, st_s.at[0], st_r.at[0], plane[1])
    state_all.wait_recv()
    state = prm_buf[24:40, :]
    for m in range(15):
        state = jnp.where(m < mine, decay_256 * state + state_buf[m], state)
    states = [state]
    for k in range(3):
        states.append(decay_64 * states[-1] + sums[k])
    collect(1)

    def advance(i, held_states):
        new = []
        for k, s in enumerate(held_states):
            at = pl.ds(pl.multiple_of(64 * k + 8 * i, 8), 8)
            some = gated_buf[at, :]
            out = []
            for j in range(8):
                s = decay * s + jnp.broadcast_to(some[j : j + 1, :], (16, 128))
                out.append(jnp.sum(res * s, axis=0, keepdims=True))
            long_buf[at, :] = jnp.concatenate(out, axis=0)
            new.append(s)
        return tuple(new)

    lax.fori_loop(0, 8, advance, tuple(states))

    join(1)
    long_rows = long_buf[...].astype(jnp.bfloat16).astype(jnp.float32)
    result = mixed(0) * (long_rows + prm_buf[15:16, :] * gated_buf[...])
    result = result.astype(jnp.bfloat16)
    home_send[0] = result[0:128, :]
    home_send[1] = result[128:256, :]

    def home_copy(q):
        return remote(home_send.at[q], home_recv.at[c], home_s.at[q], home_r.at[c], home_to[q])

    for q in range(2):
        stays = jnp.logical_and(at_home, c == q)

        @pl.when(stays)
        def _():
            home_recv[q] = home_send[q]

        @pl.when(jnp.logical_not(stays))
        def _():
            home_copy(q).start()

    all_but_one = a_buf.at[pl.ds(0, 15), 0]
    remote(all_but_one, all_but_one, ring_s.at[0], ring_r.at[0, 0, 0], z_up).wait_send()
    sib_all.wait_send()
    col_all = w_buf.at[:, pl.ds(0, 1536)]
    remote(col_all, col_all, col_s.at[0], col_r.at[0, 0, 0, 0], y_up).wait_send()
    for p in range(3):
        for h in range(2):

            @pl.when(jnp.logical_not(one_stays(h)))
            def _():
                one_copy(h, p).wait_send()

            @pl.when(jnp.logical_not(two_stays(h)))
            def _():
                two_copy(h, p).wait_send()

    for p in range(2):
        sum_all(p).wait_send()
        halo_copy(p).wait_send()

    @pl.when(away)
    def _():
        prm_copy.wait_send()

    state_all.wait_send()
    for q in range(2):

        @pl.when(jnp.logical_not(jnp.logical_and(at_home, c == q)))
        def _():
            home_copy(q).wait_send()
            remote(
                home_send.at[q], home_recv.at[q], home_s.at[q], home_r.at[q], home_to[q]
            ).wait_recv()

    for h in range(2):
        out_ref[:, 128 * h : 128 * h + 128] = home_recv[h]


def shards(
    tokens, in_weight, short_taps, carry_rows, pole_rates, residues, carry_state, skip_gain, groups
):
    vmem = pl.BlockSpec(memory_space=pltpu.VMEM)
    dma = pltpu.SemaphoreType.DMA
    bf16, f32 = jnp.bfloat16, jnp.float32
    operands = (
        tokens,
        in_weight.transpose(1, 0, 2),
        short_taps,
        carry_rows.transpose(1, 0, 2),
        pole_rates,
        residues,
        carry_state.T,
        skip_gain[None],
        groups[None],
    )
    return pl.pallas_call(
        kernel,
        out_shape=jax.ShapeDtypeStruct((128, 256), bf16),
        in_specs=[pl.BlockSpec(memory_space=pl.ANY)] * 9,
        out_specs=vmem,
        scratch_shapes=[pltpu.VMEM(a.shape, a.dtype) for a in operands]
        + [
            pltpu.VMEM((16, 2, 128, 512), bf16),
            pltpu.VMEM((2, 3, 256, 128), bf16),
            pltpu.VMEM((3, 2048, 128), bf16),
            pltpu.VMEM((3, 256, 256), bf16),
            pltpu.VMEM((3, 256, 128), bf16),
            pltpu.VMEM((3, 256, 256), bf16),
            pltpu.VMEM((3, 256, 128), bf16),
            pltpu.VMEM((40, 128), f32),
            pltpu.VMEM((40, 128), f32),
            pltpu.VMEM((128, 128), f32),
            pltpu.VMEM((4, 16, 128), f32),
            pltpu.VMEM((264, 384), f32),
            pltpu.VMEM((256, 128), f32),
            pltpu.VMEM((256, 128), f32),
            pltpu.VMEM((16, 16, 128), f32),
            pltpu.VMEM((16, 384), bf16),
            pltpu.VMEM((16, 384), bf16),
            pltpu.VMEM((2, 128, 128), bf16),
            pltpu.VMEM((2, 128, 128), bf16),
            dma((1,)),
            dma((2, 8, SUBS)),
            dma((1,)),
            dma((1,)),
            dma((2, 3)),
            dma((2, 3)),
            dma((2, 3)),
            dma((2, 3)),
            dma((1,)),
            dma((2, 2, 2, 3)),
            dma((2,)),
            dma((2,)),
            dma((1,)),
            dma((1,)),
            dma((1,)),
            dma((1,)),
            dma((2,)),
            dma((2,)),
            dma((2,)),
            dma((2,)),
            dma((9,)),
        ],
        compiler_params=pltpu.CompilerParams(
            collective_id=0, has_side_effects=True, vmem_limit_bytes=63 * 1024 * 1024
        ),
        name="operator",
    )(*operands)


def solution(mesh):
    in_specs = (
        P("seq", "mp"),
        P("seq", None, "mp"),
        P(None, None, "mp"),
        P(None, None, "mp"),
        P(),
        P(),
        P("mp", None),
        P("mp"),
        P("mp"),
    )
    out_specs = P("seq", "mp")
    return jax.shard_map(shards, mesh=mesh, in_specs=in_specs, out_specs=out_specs, check_vma=False)
```

```python
import jax
import jax.numpy as jnp
from jax import lax
from jax.experimental import pallas as pl
from jax.experimental.pallas import tpu as pltpu
from jax.sharding import PartitionSpec as P

MESH = pl.DeviceIdType.MESH
SUBS = 4
MOVE, SPREAD, FORWARD = (2, 3, 8), (4, 5, 9), (6, 7, 10)
START = (0, 0, 3)
PIECES = ((1, 1), (2, 1), (0, 1))
BRANCHES = ((1, 2), (0, 1))


def offset(pair):
    return pair // 2 * (pair - 2) + (1 - pair // 2) * (3 - pair)


def device(x, y, z, c):
    return {"seq": y * 8 + z % 8, "mp": x * 4 + (z // 8) * 2 + c}


def kernel(
    tok_in,
    w_in,
    taps_in,
    carry_in,
    pole_in,
    res_in,
    start_in,
    skip_in,
    group_in,
    out_ref,
    tok_ref,
    w_ref,
    taps_ref,
    carry_ref,
    pole_ref,
    res_ref,
    start_ref,
    skip_ref,
    group_ref,
    a_buf,
    stage_buf,
    w_buf,
    part_kv,
    part_q,
    sum_kv,
    sum_q,
    prm_send,
    prm_buf,
    turn_buf,
    mode_buf,
    ext_buf,
    gated_buf,
    long_buf,
    state_buf,
    halo_send,
    halo_recv,
    home_send,
    home_recv,
    ring_s,
    ring_r,
    sib_s,
    sib_r,
    one_s,
    one_r,
    two_s,
    two_r,
    col_s,
    col_r,
    sum_s,
    sum_r,
    st_s,
    st_r,
    prm_s,
    prm_r,
    halo_s,
    halo_r,
    home_s,
    home_r,
    in_s,
):
    taken = [
        pltpu.make_async_copy(src, dst, in_s.at[i])
        for i, (src, dst) in enumerate(
            (
                (tok_in, tok_ref),
                (w_in, w_ref),
                (taps_in, taps_ref),
                (carry_in, carry_ref),
                (pole_in, pole_ref),
                (res_in, res_ref),
                (start_in, start_ref),
                (skip_in, skip_ref),
                (group_in, group_ref),
            )
        )
    ]
    for copy in taken:
        copy.start()
    seq, mp = lax.axis_index("seq"), lax.axis_index("mp")
    y, zl = seq // 8, seq % 8
    x, zh, c = mp // 4, (mp // 2) % 2, mp % 2
    z = zh * 8 + zl

    def remote(src, dst, send, recv, to):
        return pltpu.make_async_remote_copy(
            src_ref=src,
            dst_ref=dst,
            send_sem=send,
            recv_sem=recv,
            device_id=to,
            device_id_type=MESH,
        )

    z_up, z_down = device(x, y, (z + 1) % 16, c), device(x, y, (z + 15) % 16, c)
    sibling = device(x, y, z, 1 - c)
    y_up, y_down = device(x, (y + 1) % 4, z, c), device(x, (y + 3) % 4, z, c)
    plane = [device((x + i % 4) % 4, (y + i // 4) % 4, z, c) for i in range(16)]
    turn = (zl + 8 - x - y) % 4
    one_to = [device(y, turn, z, h) for h in range(2)]
    one_from = [device(turn, x, z, h) for h in range(2)]
    two_to = [device(x, y, zh * 8 + 2 * turn + h, c) for h in range(2)]
    first = (zl // 2 + x + y) % 4
    two_from = [device(x, y, zh * 8 + first + 4 * h, c) for h in range(2)]
    own = (x + offset(zl // 2)) % 4
    home_to = [device(zl // 2, y, zh * 8 + 2 * own + q, zl % 2) for q in range(2)]
    owner = (zl // 2 + 4 - offset(x)) % 4
    home_from = [device(owner, y, zh * 8 + 2 * x + c, h) for h in range(2)]
    partner = device(owner, y, zh * 8 + 2 * x + c, zl % 2)
    at_home = jnp.logical_and(zl // 2 == x, zl == 2 * own + c)
    away = jnp.logical_not(at_home)
    one_same = jnp.logical_and(x == y, turn == y)

    barrier = pltpu.get_barrier_semaphore()
    met = home_to + home_from + two_to + two_from + one_to + one_from + plane[:0:-1]
    met = met + [z_up, z_down, sibling]
    for other in met:
        pl.semaphore_signal(barrier, inc=1, device_id=other, device_id_type=MESH)

    for copy in taken:
        copy.wait()

    def half(rows):
        return jnp.where(zl % 2 == 0, rows[:, 0:128], rows[:, 128:256])

    for tap in range(3):
        prm_send[3 * tap : 3 * tap + 3, :] = half(taps_ref[tap])
    for b in range(3):
        pair = half(carry_ref[b].astype(jnp.float32))
        for i in range(2):
            prm_send[9 + 3 * i + b : 10 + 3 * i + b, :] = pair[i : i + 1, :]
    prm_send[15:16, :] = half(skip_ref[...])
    prm_send[16:17, :] = half(group_ref[...].astype(jnp.float32))
    prm_send[17:24, :] = jnp.zeros((7, 128), jnp.float32)
    prm_send[24:40, :] = half(start_ref[...])
    turn_buf[...] = jnp.zeros((128, 128), jnp.float32)
    turn_buf[0:16, 0:16] = pole_ref[...]
    turn_buf[16:32, 0:16] = res_ref[...]
    turn_buf[...] = jnp.transpose(turn_buf[...])

    pl.semaphore_wait(barrier, len(met))

    def one_copy(h, p, landed=None):
        some = pl.ds(*PIECES[p])
        at = c if landed is None else landed
        src = w_ref.at[some, :, pl.ds(h * 128, 128)]
        return remote(src, stage_buf.at[at, some], one_s.at[h, p], one_r.at[at, p], one_to[h])

    def one_stays(h):
        return jnp.logical_and(one_same, c == h)

    def set_out(p):
        for h in range(2):

            @pl.when(jnp.logical_not(one_stays(h)))
            def _():
                one_copy(h, p).start()

    for p in range(3):
        if START[p] == 0:
            set_out(p)

    rows = 128 // SUBS

    def held(way, t):
        return (z + 16 - t) % 16 if way == 0 else (z + t) % 16

    def ring_copy(way, t, u):
        part = pl.ds(u * rows, rows)
        dst = a_buf.at[held(way, t), c, part]
        src = tok_ref.at[part] if t == 0 else dst
        to = z_up if way == 0 else z_down
        return remote(src, dst, ring_s.at[0], ring_r.at[way, t, u], to)

    def sib_copy(way, t):
        part = pl.ds(0, 128) if t < 8 else pl.ds(64 * way, 64)
        dst = a_buf.at[held(way, t), c, part]
        src = tok_ref if t == 0 else dst
        return remote(src, dst, sib_s.at[0], sib_r.at[0], sibling)

    def uses(way, t):
        if t < 7:
            return range(SUBS)
        return range(SUBS // 2) if way == 0 else range(SUBS // 2, SUBS)

    for u in range(SUBS):
        for way in range(2):
            copy = ring_copy(way, 0, u)
            copy.start()
    sib_copy(0, 0).start()

    prm_copy = remote(prm_send, prm_buf, prm_s.at[0], prm_r.at[0], partner)

    @pl.when(away)
    def _():
        prm_copy.start()

    @pl.when(at_home)
    def _():
        prm_buf[...] = prm_send[...]

    a_buf[z, c] = tok_ref[...]
    for h in range(2):

        @pl.when(one_stays(h))
        def _():
            stage_buf[h] = w_ref[:, :, h * 128 : h * 128 + 128]

    def block(index, p):
        at = pl.ds(pl.multiple_of(index * 256, 256), 256)
        return w_buf.at[pl.ds(*PIECES[p]), at]

    def two_copy(h, p):
        src = stage_buf.at[h, pl.ds(*PIECES[p])]
        return remote(src, block(zl, p), two_s.at[h, p], two_r.at[zl // 4, p], two_to[h])

    def two_stays(h):
        return zl == 2 * turn + h

    def move(h, p):
        @pl.when(jnp.logical_not(one_stays(h)))
        def _():
            one_copy(h, p, h).wait_recv()

        @pl.when(two_stays(h))
        def _():
            low, count = PIECES[p]
            at = pl.ds(pl.multiple_of(zl * 256, 256), 256)
            for b in range(low, low + count):
                w_buf[b, at, :] = stage_buf[h, b]

        @pl.when(jnp.logical_not(two_stays(h)))
        def _():
            two_copy(h, p).start()

    def col_copy(way, hop, h, p):
        step = hop if way == 0 else -hop
        ref = block((first + 4 - step) % 4 + 4 * h, p)
        to = y_up if way == 0 else y_down
        return remote(ref, ref, col_s.at[0], col_r.at[way, hop, h, p], to)

    def spread(h, p):
        @pl.when(zl != first + 4 * h)
        def _():
            src = stage_buf.at[h, pl.ds(*PIECES[p])]
            dst = block(first + 4 * h, p)
            remote(src, dst, two_s.at[h, p], two_r.at[h, p], two_to[h]).wait_recv()

        for way in range(2):
            col_copy(way, 0, h, p).start()

    def forward(way, p):
        col_copy(way, 0, way, p).wait_recv()
        col_copy(way, 1, way, p).start()

    def gathered(p):
        for way in range(2):
            col_copy(way, 0, 1 - way, p).wait_recv()
            col_copy(way, 1, way, p).wait_recv()

    def weights_at(t):
        for p in range(3):
            for h in range(2):
                if t == MOVE[p]:
                    move(h, p)
            if t == START[p]:
                set_out(p)
            for h in range(2):
                if t == SPREAD[p]:
                    spread(h, p)
            for h in range(2):
                if t == FORWARD[p]:
                    forward(h, p)

    def modes():
        @pl.when(away)
        def _():
            prm_copy.wait_recv()

        groups = prm_buf[16:17, :]
        rates = jnp.zeros((16, 128), jnp.float32)
        res = jnp.zeros((16, 128), jnp.float32)
        for g in range(16):
            here = groups == float(g)
            rates = jnp.where(here, turn_buf[0:16, g : g + 1], rates)
            res = jnp.where(here, turn_buf[0:16, 16 + g : 17 + g], res)
        mode_buf[0] = jnp.exp(-rates)
        mode_buf[1] = jnp.exp(-64.0 * rates)
        mode_buf[2] = jnp.exp(-256.0 * rates)
        mode_buf[3] = res

    for t in range(1, 9):
        for u in range(SUBS):
            for way in range(2):
                if u in uses(way, t - 1):
                    ring_copy(way, t - 1, u).wait_recv()
                    if t < 8 and u in uses(way, t):
                        copy = ring_copy(way, t, u)
                        copy.start()
        for way in range(2):
            sib_copy(way, t).start()
        weights_at(t)
        if t == 5:
            modes()
    gathered(0)
    gathered(1)
    shards_of = a_buf.at[:, 0]
    sib_all = remote(shards_of, shards_of, sib_s.at[0], sib_r.at[0], sibling)
    sib_all.wait_recv()

    def sum_copy(p, k):
        part, to_buf = ((part_kv, sum_kv), (part_q, sum_q))[p]
        to = (x + 1 + k) % 4
        return remote(
            part.at[k], to_buf.at[k], sum_s.at[p], sum_r.at[p], device(to, y, z, c)
        )

    def product(p, to):
        total = None
        for side in range(2):
            for core in range(2):
                at = slice((side * 4 + core * 2) * 256, (side * 4 + core * 2) * 256 + 512)
                left = a_buf[pl.ds(side * 8 + 2 * ((to + offset(zl // 2)) % 4), 2), core].reshape(256, 512)
                if p == 0:
                    right = jnp.concatenate([w_buf[1, at, :], w_buf[2, at, :]], axis=1)
                else:
                    right = w_buf[0, at, :]
                term = jnp.dot(left, right, preferred_element_type=jnp.float32)
                total = term if total is None else total + term
        return total

    def sum_all(p):
        part, to_buf = ((part_kv, sum_kv), (part_q, sum_q))[p]
        return remote(part, to_buf, sum_s.at[p], sum_r.at[p], plane[1])

    lanes_of = (slice(128, 384), slice(0, 128))

    def products(p):
        part = (part_kv, part_q)[p]

        @pl.loop(1, 4)
        def _(turned):
            k = turned % 3
            part[k] = product(p, (x + 1 + k) % 4).astype(jnp.bfloat16)
            sum_copy(p, k).start()

        ext_buf[8:264, lanes_of[p]] = product(p, x)

    halo_to = device((x + 1) % 4, (y + (own + 1) // 4) % 4, z, c)
    is_first = jnp.logical_and(own == 0, y == 0)

    def halo_copy(p):
        part = pl.ds(lanes_of[p].start, lanes_of[p].stop - lanes_of[p].start)
        return remote(
            halo_send.at[:, part], halo_recv.at[:, part], halo_s.at[p], halo_r.at[p], halo_to
        )

    def collect(p):
        got = (sum_kv, sum_q)[p]
        total = ext_buf[8:264, lanes_of[p]]
        sum_all(p).wait_recv()
        for k in range(3):
            total += got[k].astype(jnp.float32)
        rounded = total.astype(jnp.bfloat16)
        halo_send[:, lanes_of[p]] = rounded[240:256, :]
        halo_copy(p).start()
        ext_buf[8:264, lanes_of[p]] = rounded.astype(jnp.float32)

    def join(p):
        halo_copy(p).wait_recv()
        low, count = BRANCHES[p]
        for b in range(low, low + count):
            lanes = slice(128 * b, 128 * b + 128)
            last = halo_recv[:, lanes].astype(jnp.float32)
            for i in range(2):
                carried = prm_buf[9 + 3 * i + b : 10 + 3 * i + b, :]
                ext_buf[6 + i : 7 + i, lanes] = jnp.where(
                    is_first, carried, last[14 + i : 15 + i, :]
                )

    def mixed(b):
        lanes = slice(128 * b, 128 * b + 128)
        return (
            prm_buf[b : b + 1, :] * ext_buf[8:264, lanes]
            + prm_buf[3 + b : 4 + b, :] * ext_buf[7:263, lanes]
            + prm_buf[6 + b : 7 + b, :] * ext_buf[6:262, lanes]
        )

    products(0)
    weights_at(8 + 1)
    collect(0)
    weights_at(8 + 2)
    join(0)
    gated_buf[...] = (mixed(1) * mixed(2)).astype(jnp.bfloat16).astype(jnp.float32)

    decay, decay_64, decay_256, res = [mode_buf[i] for i in range(4)]

    def leave(i, sums):
        new = []
        for k, s in enumerate(sums):
            some = gated_buf[pl.ds(pl.multiple_of(64 * k + 8 * i, 8), 8), :]
            for j in range(8):
                s = decay * s + jnp.broadcast_to(some[j : j + 1, :], (16, 128))
            new.append(s)
        return tuple(new)

    zero = jnp.zeros((16, 128), jnp.float32)
    sums = lax.fori_loop(0, 8, leave, (zero,) * 4)
    mine = 4 * y + own
    state_buf[mine] = sums[3] + decay_64 * (
        sums[2] + decay_64 * (sums[1] + decay_64 * sums[0])
    )

    def state_copy(i):
        here = state_buf.at[mine]
        return remote(here, here, st_s.at[0], st_r.at[0], plane[i])

    for i in range(1, 16):
        state_copy(i).start()

    gathered(2)
    products(1)

    others = state_buf.at[pl.ds(0, 15)]
    state_all = remote(others, others, st_s.at[0], st_r.at[0], plane[1])
    state_all.wait_recv()
    state = prm_buf[24:40, :]
    for m in range(15):
        state = jnp.where(m < mine, decay_256 * state + state_buf[m], state)
    states = [state]
    for k in range(3):
        states.append(decay_64 * states[-1] + sums[k])
    collect(1)

    def advance(i, held_states):
        new = []
        for k, s in enumerate(held_states):
            at = pl.ds(pl.multiple_of(64 * k + 8 * i, 8), 8)
            some = gated_buf[at, :]
            out = []
            for j in range(8):
                s = decay * s + jnp.broadcast_to(some[j : j + 1, :], (16, 128))
                out.append(jnp.sum(res * s, axis=0, keepdims=True))
            long_buf[at, :] = jnp.concatenate(out, axis=0)
            new.append(s)
        return tuple(new)

    lax.fori_loop(0, 8, advance, tuple(states))

    join(1)
    long_rows = long_buf[...].astype(jnp.bfloat16).astype(jnp.float32)
    result = mixed(0) * (long_rows + prm_buf[15:16, :] * gated_buf[...])
    result = result.astype(jnp.bfloat16)
    home_send[0] = result[0:128, :]
    home_send[1] = result[128:256, :]

    def home_copy(q):
        return remote(home_send.at[q], home_recv.at[c], home_s.at[q], home_r.at[c], home_to[q])

    for q in range(2):
        stays = jnp.logical_and(at_home, c == q)

        @pl.when(stays)
        def _():
            home_recv[q] = home_send[q]

        @pl.when(jnp.logical_not(stays))
        def _():
            home_copy(q).start()

    all_but_one = a_buf.at[pl.ds(0, 15), 0]
    remote(all_but_one, all_but_one, ring_s.at[0], ring_r.at[0, 0, 0], z_up).wait_send()
    sib_all.wait_send()
    col_all = w_buf.at[:, pl.ds(0, 1536)]
    remote(col_all, col_all, col_s.at[0], col_r.at[0, 0, 0, 0], y_up).wait_send()
    for p in range(3):
        for h in range(2):

            @pl.when(jnp.logical_not(one_stays(h)))
            def _():
                one_copy(h, p).wait_send()

            @pl.when(jnp.logical_not(two_stays(h)))
            def _():
                two_copy(h, p).wait_send()

    for p in range(2):
        sum_all(p).wait_send()
        halo_copy(p).wait_send()

    @pl.when(away)
    def _():
        prm_copy.wait_send()

    state_all.wait_send()
    for q in range(2):

        @pl.when(jnp.logical_not(jnp.logical_and(at_home, c == q)))
        def _():
            home_copy(q).wait_send()
            remote(
                home_send.at[q], home_recv.at[q], home_s.at[q], home_r.at[q], home_to[q]
            ).wait_recv()

    for h in range(2):
        out_ref[:, 128 * h : 128 * h + 128] = home_recv[h]


def shards(
    tokens, in_weight, short_taps, carry_rows, pole_rates, residues, carry_state, skip_gain, groups
):
    vmem = pl.BlockSpec(memory_space=pltpu.VMEM)
    dma = pltpu.SemaphoreType.DMA
    bf16, f32 = jnp.bfloat16, jnp.float32
    operands = (
        tokens,
        in_weight.transpose(1, 0, 2),
        short_taps,
        carry_rows.transpose(1, 0, 2),
        pole_rates,
        residues,
        carry_state.T,
        skip_gain[None],
        groups[None],
    )
    return pl.pallas_call(
        kernel,
        out_shape=jax.ShapeDtypeStruct((128, 256), bf16),
        in_specs=[pl.BlockSpec(memory_space=pl.ANY)] * 9,
        out_specs=vmem,
        scratch_shapes=[pltpu.VMEM(a.shape, a.dtype) for a in operands]
        + [
            pltpu.VMEM((16, 2, 128, 512), bf16),
            pltpu.VMEM((2, 3, 256, 128), bf16),
            pltpu.VMEM((3, 2048, 128), bf16),
            pltpu.VMEM((3, 256, 256), bf16),
            pltpu.VMEM((3, 256, 128), bf16),
            pltpu.VMEM((3, 256, 256), bf16),
            pltpu.VMEM((3, 256, 128), bf16),
            pltpu.VMEM((40, 128), f32),
            pltpu.VMEM((40, 128), f32),
            pltpu.VMEM((128, 128), f32),
            pltpu.VMEM((4, 16, 128), f32),
            pltpu.VMEM((264, 384), f32),
            pltpu.VMEM((256, 128), f32),
            pltpu.VMEM((256, 128), f32),
            pltpu.VMEM((16, 16, 128), f32),
            pltpu.VMEM((16, 384), bf16),
            pltpu.VMEM((16, 384), bf16),
            pltpu.VMEM((2, 128, 128), bf16),
            pltpu.VMEM((2, 128, 128), bf16),
            dma((1,)),
            dma((2, 8, SUBS)),
            dma((1,)),
            dma((1,)),
            dma((2, 3)),
            dma((2, 3)),
            dma((2, 3)),
            dma((2, 3)),
            dma((1,)),
            dma((2, 2, 2, 3)),
            dma((2,)),
            dma((2,)),
            dma((1,)),
            dma((1,)),
            dma((1,)),
            dma((1,)),
            dma((2,)),
            dma((2,)),
            dma((2,)),
            dma((2,)),
            dma((9,)),
        ],
        compiler_params=pltpu.CompilerParams(
            collective_id=0, has_side_effects=True, vmem_limit_bytes=63 * 1024 * 1024
        ),
        name="operator",
    )(*operands)


def solution(mesh):
    in_specs = (
        P("seq", "mp"),
        P("seq", None, "mp"),
        P(None, None, "mp"),
        P(None, None, "mp"),
        P(),
        P(),
        P("mp", None),
        P("mp"),
        P("mp"),
    )
    out_specs = P("seq", "mp")
    return jax.shard_map(shards, mesh=mesh, in_specs=in_specs, out_specs=out_specs, check_vma=False)
```

```python
import jax
import jax.numpy as jnp
from jax import lax
from jax.experimental import pallas as pl
from jax.experimental.pallas import tpu as pltpu
from jax.sharding import PartitionSpec as P

MESH = pl.DeviceIdType.MESH
SUBS = 4
MOVE, SPREAD, FORWARD = (2, 3, 8), (4, 5, 9), (6, 7, 10)
START = (0, 0, 3)
PIECES = ((1, 1), (2, 1), (0, 1))
BRANCHES = ((1, 2), (0, 1))


def offset(pair):
    return pair // 2 * (pair - 2) + (1 - pair // 2) * (3 - pair)


def device(x, y, z, c):
    return {"seq": y * 8 + z % 8, "mp": x * 4 + (z // 8) * 2 + c}


def kernel(
    tok_in,
    w_in,
    taps_in,
    carry_in,
    pole_in,
    res_in,
    start_in,
    skip_in,
    group_in,
    out_ref,
    tok_ref,
    w_ref,
    taps_ref,
    carry_ref,
    pole_ref,
    res_ref,
    start_ref,
    skip_ref,
    group_ref,
    a_buf,
    stage_buf,
    w_buf,
    part_kv,
    part_q,
    sum_kv,
    sum_q,
    prm_send,
    prm_buf,
    turn_buf,
    mode_buf,
    ext_buf,
    gated_buf,
    long_buf,
    state_buf,
    halo_send,
    halo_recv,
    home_send,
    home_recv,
    ring_s,
    ring_r,
    sib_s,
    sib_r,
    one_s,
    one_r,
    two_s,
    two_r,
    col_s,
    col_r,
    sum_s,
    sum_r,
    st_s,
    st_r,
    prm_s,
    prm_r,
    halo_s,
    halo_r,
    home_s,
    home_r,
    in_s,
):
    taken = [
        pltpu.make_async_copy(src, dst, in_s.at[i])
        for i, (src, dst) in enumerate(
            (
                (tok_in, tok_ref),
                (w_in, w_ref),
                (taps_in, taps_ref),
                (carry_in, carry_ref),
                (pole_in, pole_ref),
                (res_in, res_ref),
                (start_in, start_ref),
                (skip_in, skip_ref),
                (group_in, group_ref),
            )
        )
    ]
    for copy in taken:
        copy.start()
    seq, mp = lax.axis_index("seq"), lax.axis_index("mp")
    y, zl = seq // 8, seq % 8
    x, zh, c = mp // 4, (mp // 2) % 2, mp % 2
    z = zh * 8 + zl

    def remote(src, dst, send, recv, to):
        return pltpu.make_async_remote_copy(
            src_ref=src,
            dst_ref=dst,
            send_sem=send,
            recv_sem=recv,
            device_id=to,
            device_id_type=MESH,
        )

    z_up, z_down = device(x, y, (z + 1) % 16, c), device(x, y, (z + 15) % 16, c)
    sibling = device(x, y, z, 1 - c)
    y_up, y_down = device(x, (y + 1) % 4, z, c), device(x, (y + 3) % 4, z, c)
    plane = [device((x + i % 4) % 4, (y + i // 4) % 4, z, c) for i in range(16)]
    turn = (zl + 8 - x - y) % 4
    one_to = [device(y, turn, z, h) for h in range(2)]
    one_from = [device(turn, x, z, h) for h in range(2)]
    two_to = [device(x, y, zh * 8 + 2 * turn + h, c) for h in range(2)]
    first = (zl // 2 + x + y) % 4
    two_from = [device(x, y, zh * 8 + first + 4 * h, c) for h in range(2)]
    own = (x + offset(zl // 2)) % 4
    home_to = [device(zl // 2, y, zh * 8 + 2 * own + q, zl % 2) for q in range(2)]
    owner = (zl // 2 + 4 - offset(x)) % 4
    home_from = [device(owner, y, zh * 8 + 2 * x + c, h) for h in range(2)]
    partner = device(owner, y, zh * 8 + 2 * x + c, zl % 2)
    at_home = jnp.logical_and(zl // 2 == x, zl == 2 * own + c)
    away = jnp.logical_not(at_home)
    one_same = jnp.logical_and(x == y, turn == y)

    barrier = pltpu.get_barrier_semaphore()
    met = home_to + home_from + two_to + two_from + one_to + one_from + plane[:0:-1]
    met = met + [z_up, z_down, sibling]
    for other in met:
        pl.semaphore_signal(barrier, inc=1, device_id=other, device_id_type=MESH)

    for copy in taken:
        copy.wait()

    def half(rows):
        return jnp.where(zl % 2 == 0, rows[:, 0:128], rows[:, 128:256])

    for tap in range(3):
        prm_send[3 * tap : 3 * tap + 3, :] = half(taps_ref[tap])
    for b in range(3):
        pair = half(carry_ref[b].astype(jnp.float32))
        for i in range(2):
            prm_send[9 + 3 * i + b : 10 + 3 * i + b, :] = pair[i : i + 1, :]
    prm_send[15:16, :] = half(skip_ref[...])
    prm_send[16:17, :] = half(group_ref[...].astype(jnp.float32))
    prm_send[17:24, :] = jnp.zeros((7, 128), jnp.float32)
    prm_send[24:40, :] = half(start_ref[...])
    turn_buf[...] = jnp.zeros((128, 128), jnp.float32)
    turn_buf[0:16, 0:16] = pole_ref[...]
    turn_buf[16:32, 0:16] = res_ref[...]
    turn_buf[...] = jnp.transpose(turn_buf[...])

    pl.semaphore_wait(barrier, len(met))

    def one_copy(h, p, landed=None):
        some = pl.ds(*PIECES[p])
        at = c if landed is None else landed
        src = w_ref.at[some, :, pl.ds(h * 128, 128)]
        return remote(src, stage_buf.at[at, some], one_s.at[h, p], one_r.at[at, p], one_to[h])

    def one_stays(h):
        return jnp.logical_and(one_same, c == h)

    def set_out(p):
        for h in range(2):

            @pl.when(jnp.logical_not(one_stays(h)))
            def _():
                one_copy(h, p).start()


    rows = 128 // SUBS

    def held(way, t):
        return (z + 16 - t) % 16 if way == 0 else (z + t) % 16

    def ring_copy(way, t, u):
        part = pl.ds(u * rows, rows)
        dst = a_buf.at[held(way, t), c, part]
        src = tok_ref.at[part] if t == 0 else dst
        to = z_up if way == 0 else z_down
        return remote(src, dst, ring_s.at[0], ring_r.at[way, t, u], to)

    def sib_copy(way, t):
        part = pl.ds(0, 128) if t < 8 else pl.ds(64 * way, 64)
        dst = a_buf.at[held(way, t), c, part]
        src = tok_ref if t == 0 else dst
        return remote(src, dst, sib_s.at[0], sib_r.at[0], sibling)

    def uses(way, t):
        if t < 7:
            return range(SUBS)
        return range(SUBS // 2) if way == 0 else range(SUBS // 2, SUBS)

    for u in range(SUBS):
        for way in range(2):
            copy = ring_copy(way, 0, u)
            copy.start()
    sib_copy(0, 0).start()

    for p in range(3):
        if START[p] == 0:
            set_out(p)
    prm_copy = remote(prm_send, prm_buf, prm_s.at[0], prm_r.at[0], partner)

    @pl.when(away)
    def _():
        prm_copy.start()

    @pl.when(at_home)
    def _():
        prm_buf[...] = prm_send[...]

    a_buf[z, c] = tok_ref[...]
    for h in range(2):

        @pl.when(one_stays(h))
        def _():
            stage_buf[h] = w_ref[:, :, h * 128 : h * 128 + 128]

    def block(index, p):
        at = pl.ds(pl.multiple_of(index * 256, 256), 256)
        return w_buf.at[pl.ds(*PIECES[p]), at]

    def two_copy(h, p):
        src = stage_buf.at[h, pl.ds(*PIECES[p])]
        return remote(src, block(zl, p), two_s.at[h, p], two_r.at[zl // 4, p], two_to[h])

    def two_stays(h):
        return zl == 2 * turn + h

    def move(h, p):
        @pl.when(jnp.logical_not(one_stays(h)))
        def _():
            one_copy(h, p, h).wait_recv()

        @pl.when(two_stays(h))
        def _():
            low, count = PIECES[p]
            at = pl.ds(pl.multiple_of(zl * 256, 256), 256)
            for b in range(low, low + count):
                w_buf[b, at, :] = stage_buf[h, b]

        @pl.when(jnp.logical_not(two_stays(h)))
        def _():
            two_copy(h, p).start()

    def col_copy(way, hop, h, p):
        step = hop if way == 0 else -hop
        ref = block((first + 4 - step) % 4 + 4 * h, p)
        to = y_up if way == 0 else y_down
        return remote(ref, ref, col_s.at[0], col_r.at[way, hop, h, p], to)

    def spread(h, p):
        @pl.when(zl != first + 4 * h)
        def _():
            src = stage_buf.at[h, pl.ds(*PIECES[p])]
            dst = block(first + 4 * h, p)
            remote(src, dst, two_s.at[h, p], two_r.at[h, p], two_to[h]).wait_recv()

        for way in range(2):
            col_copy(way, 0, h, p).start()

    def forward(way, p):
        col_copy(way, 0, way, p).wait_recv()
        col_copy(way, 1, way, p).start()

    def gathered(p):
        for way in range(2):
            col_copy(way, 0, 1 - way, p).wait_recv()
            col_copy(way, 1, way, p).wait_recv()

    def weights_at(t):
        for p in range(3):
            for h in range(2):
                if t == MOVE[p]:
                    move(h, p)
            if t == START[p]:
                set_out(p)
            for h in range(2):
                if t == SPREAD[p]:
                    spread(h, p)
            for h in range(2):
                if t == FORWARD[p]:
                    forward(h, p)

    def modes():
        @pl.when(away)
        def _():
            prm_copy.wait_recv()

        groups = prm_buf[16:17, :]
        rates = jnp.zeros((16, 128), jnp.float32)
        res = jnp.zeros((16, 128), jnp.float32)
        for g in range(16):
            here = groups == float(g)
            rates = jnp.where(here, turn_buf[0:16, g : g + 1], rates)
            res = jnp.where(here, turn_buf[0:16, 16 + g : 17 + g], res)
        mode_buf[0] = jnp.exp(-rates)
        mode_buf[1] = jnp.exp(-64.0 * rates)
        mode_buf[2] = jnp.exp(-256.0 * rates)
        mode_buf[3] = res

    for t in range(1, 9):
        for u in range(SUBS):
            for way in range(2):
                if u in uses(way, t - 1):
                    ring_copy(way, t - 1, u).wait_recv()
                    if t < 8 and u in uses(way, t):
                        copy = ring_copy(way, t, u)
                        copy.start()
        for way in range(2):
            sib_copy(way, t).start()
        weights_at(t)
        if t == 5:
            modes()
    gathered(0)
    gathered(1)
    shards_of = a_buf.at[:, 0]
    sib_all = remote(shards_of, shards_of, sib_s.at[0], sib_r.at[0], sibling)
    sib_all.wait_recv()

    def sum_copy(p, k):
        part, to_buf = ((part_kv, sum_kv), (part_q, sum_q))[p]
        to = (x + 1 + k) % 4
        return remote(
            part.at[k], to_buf.at[k], sum_s.at[p], sum_r.at[p], device(to, y, z, c)
        )

    def product(p, to):
        total = None
        for side in range(2):
            for core in range(2):
                at = slice((side * 4 + core * 2) * 256, (side * 4 + core * 2) * 256 + 512)
                left = a_buf[pl.ds(side * 8 + 2 * ((to + offset(zl // 2)) % 4), 2), core].reshape(256, 512)
                if p == 0:
                    right = jnp.concatenate([w_buf[1, at, :], w_buf[2, at, :]], axis=1)
                else:
                    right = w_buf[0, at, :]
                term = jnp.dot(left, right, preferred_element_type=jnp.float32)
                total = term if total is None else total + term
        return total

    def sum_all(p):
        part, to_buf = ((part_kv, sum_kv), (part_q, sum_q))[p]
        return remote(part, to_buf, sum_s.at[p], sum_r.at[p], plane[1])

    lanes_of = (slice(128, 384), slice(0, 128))

    def products(p):
        part = (part_kv, part_q)[p]

        @pl.loop(1, 4)
        def _(turned):
            k = turned % 3
            part[k] = product(p, (x + 1 + k) % 4).astype(jnp.bfloat16)
            sum_copy(p, k).start()

        ext_buf[8:264, lanes_of[p]] = product(p, x)

    halo_to = device((x + 1) % 4, (y + (own + 1) // 4) % 4, z, c)
    is_first = jnp.logical_and(own == 0, y == 0)

    def halo_copy(p):
        part = pl.ds(lanes_of[p].start, lanes_of[p].stop - lanes_of[p].start)
        return remote(
            halo_send.at[:, part], halo_recv.at[:, part], halo_s.at[p], halo_r.at[p], halo_to
        )

    def collect(p):
        got = (sum_kv, sum_q)[p]
        total = ext_buf[8:264, lanes_of[p]]
        sum_all(p).wait_recv()
        for k in range(3):
            total += got[k].astype(jnp.float32)
        rounded = total.astype(jnp.bfloat16)
        halo_send[:, lanes_of[p]] = rounded[240:256, :]
        halo_copy(p).start()
        ext_buf[8:264, lanes_of[p]] = rounded.astype(jnp.float32)

    def join(p):
        halo_copy(p).wait_recv()
        low, count = BRANCHES[p]
        for b in range(low, low + count):
            lanes = slice(128 * b, 128 * b + 128)
            last = halo_recv[:, lanes].astype(jnp.float32)
            for i in range(2):
                carried = prm_buf[9 + 3 * i + b : 10 + 3 * i + b, :]
                ext_buf[6 + i : 7 + i, lanes] = jnp.where(
                    is_first, carried, last[14 + i : 15 + i, :]
                )

    def mixed(b):
        lanes = slice(128 * b, 128 * b + 128)
        return (
            prm_buf[b : b + 1, :] * ext_buf[8:264, lanes]
            + prm_buf[3 + b : 4 + b, :] * ext_buf[7:263, lanes]
            + prm_buf[6 + b : 7 + b, :] * ext_buf[6:262, lanes]
        )

    products(0)
    weights_at(8 + 1)
    collect(0)
    weights_at(8 + 2)
    join(0)
    gated_buf[...] = (mixed(1) * mixed(2)).astype(jnp.bfloat16).astype(jnp.float32)

    decay, decay_64, decay_256, res = [mode_buf[i] for i in range(4)]

    def leave(i, sums):
        new = []
        for k, s in enumerate(sums):
            some = gated_buf[pl.ds(pl.multiple_of(64 * k + 8 * i, 8), 8), :]
            for j in range(8):
                s = decay * s + jnp.broadcast_to(some[j : j + 1, :], (16, 128))
            new.append(s)
        return tuple(new)

    zero = jnp.zeros((16, 128), jnp.float32)
    sums = lax.fori_loop(0, 8, leave, (zero,) * 4)
    mine = 4 * y + own
    state_buf[mine] = sums[3] + decay_64 * (
        sums[2] + decay_64 * (sums[1] + decay_64 * sums[0])
    )

    def state_copy(i):
        here = state_buf.at[mine]
        return remote(here, here, st_s.at[0], st_r.at[0], plane[i])

    for i in range(1, 16):
        state_copy(i).start()

    gathered(2)
    products(1)

    others = state_buf.at[pl.ds(0, 15)]
    state_all = remote(others, others, st_s.at[0], st_r.at[0], plane[1])
    state_all.wait_recv()
    state = prm_buf[24:40, :]
    for m in range(15):
        state = jnp.where(m < mine, decay_256 * state + state_buf[m], state)
    states = [state]
    for k in range(3):
        states.append(decay_64 * states[-1] + sums[k])
    collect(1)

    def advance(i, held_states):
        new = []
        for k, s in enumerate(held_states):
            at = pl.ds(pl.multiple_of(64 * k + 8 * i, 8), 8)
            some = gated_buf[at, :]
            out = []
            for j in range(8):
                s = decay * s + jnp.broadcast_to(some[j : j + 1, :], (16, 128))
                out.append(jnp.sum(res * s, axis=0, keepdims=True))
            long_buf[at, :] = jnp.concatenate(out, axis=0)
            new.append(s)
        return tuple(new)

    lax.fori_loop(0, 8, advance, tuple(states))

    join(1)
    long_rows = long_buf[...].astype(jnp.bfloat16).astype(jnp.float32)
    result = mixed(0) * (long_rows + prm_buf[15:16, :] * gated_buf[...])
    result = result.astype(jnp.bfloat16)
    home_send[0] = result[0:128, :]
    home_send[1] = result[128:256, :]

    def home_copy(q):
        return remote(home_send.at[q], home_recv.at[c], home_s.at[q], home_r.at[c], home_to[q])

    for q in range(2):
        stays = jnp.logical_and(at_home, c == q)

        @pl.when(stays)
        def _():
            home_recv[q] = home_send[q]

        @pl.when(jnp.logical_not(stays))
        def _():
            home_copy(q).start()

    all_but_one = a_buf.at[pl.ds(0, 15), 0]
    remote(all_but_one, all_but_one, ring_s.at[0], ring_r.at[0, 0, 0], z_up).wait_send()
    sib_all.wait_send()
    col_all = w_buf.at[:, pl.ds(0, 1536)]
    remote(col_all, col_all, col_s.at[0], col_r.at[0, 0, 0, 0], y_up).wait_send()
    for p in range(3):
        for h in range(2):

            @pl.when(jnp.logical_not(one_stays(h)))
            def _():
                one_copy(h, p).wait_send()

            @pl.when(jnp.logical_not(two_stays(h)))
            def _():
                two_copy(h, p).wait_send()

    for p in range(2):
        sum_all(p).wait_send()
        halo_copy(p).wait_send()

    @pl.when(away)
    def _():
        prm_copy.wait_send()

    state_all.wait_send()
    for q in range(2):

        @pl.when(jnp.logical_not(jnp.logical_and(at_home, c == q)))
        def _():
            home_copy(q).wait_send()
            remote(
                home_send.at[q], home_recv.at[q], home_s.at[q], home_r.at[q], home_to[q]
            ).wait_recv()

    for h in range(2):
        out_ref[:, 128 * h : 128 * h + 128] = home_recv[h]


def shards(
    tokens, in_weight, short_taps, carry_rows, pole_rates, residues, carry_state, skip_gain, groups
):
    vmem = pl.BlockSpec(memory_space=pltpu.VMEM)
    dma = pltpu.SemaphoreType.DMA
    bf16, f32 = jnp.bfloat16, jnp.float32
    operands = (
        tokens,
        in_weight.transpose(1, 0, 2),
        short_taps,
        carry_rows.transpose(1, 0, 2),
        pole_rates,
        residues,
        carry_state.T,
        skip_gain[None],
        groups[None],
    )
    return pl.pallas_call(
        kernel,
        out_shape=jax.ShapeDtypeStruct((128, 256), bf16),
        in_specs=[pl.BlockSpec(memory_space=pl.ANY)] * 9,
        out_specs=vmem,
        scratch_shapes=[pltpu.VMEM(a.shape, a.dtype) for a in operands]
        + [
            pltpu.VMEM((16, 2, 128, 512), bf16),
            pltpu.VMEM((2, 3, 256, 128), bf16),
            pltpu.VMEM((3, 2048, 128), bf16),
            pltpu.VMEM((3, 256, 256), bf16),
            pltpu.VMEM((3, 256, 128), bf16),
            pltpu.VMEM((3, 256, 256), bf16),
            pltpu.VMEM((3, 256, 128), bf16),
            pltpu.VMEM((40, 128), f32),
            pltpu.VMEM((40, 128), f32),
            pltpu.VMEM((128, 128), f32),
            pltpu.VMEM((4, 16, 128), f32),
            pltpu.VMEM((264, 384), f32),
            pltpu.VMEM((256, 128), f32),
            pltpu.VMEM((256, 128), f32),
            pltpu.VMEM((16, 16, 128), f32),
            pltpu.VMEM((16, 384), bf16),
            pltpu.VMEM((16, 384), bf16),
            pltpu.VMEM((2, 128, 128), bf16),
            pltpu.VMEM((2, 128, 128), bf16),
            dma((1,)),
            dma((2, 8, SUBS)),
            dma((1,)),
            dma((1,)),
            dma((2, 3)),
            dma((2, 3)),
            dma((2, 3)),
            dma((2, 3)),
            dma((1,)),
            dma((2, 2, 2, 3)),
            dma((2,)),
            dma((2,)),
            dma((1,)),
            dma((1,)),
            dma((1,)),
            dma((1,)),
            dma((2,)),
            dma((2,)),
            dma((2,)),
            dma((2,)),
            dma((9,)),
        ],
        compiler_params=pltpu.CompilerParams(
            collective_id=0, has_side_effects=True, vmem_limit_bytes=63 * 1024 * 1024
        ),
        name="operator",
    )(*operands)


def solution(mesh):
    in_specs = (
        P("seq", "mp"),
        P("seq", None, "mp"),
        P(None, None, "mp"),
        P(None, None, "mp"),
        P(),
        P(),
        P("mp", None),
        P("mp"),
        P("mp"),
    )
    out_specs = P("seq", "mp")
    return jax.shard_map(shards, mesh=mesh, in_specs=in_specs, out_specs=out_specs, check_vma=False)
```
